256 devices in a mesh: seq: 64 (over z, y, core), head: 4 (over x).
Axes of the slice: x: 4, y: 4, z: 8, core: 2. Of those that a mesh axis runs over, the one named last changes fastest.
Arguments:
- query: bfloat16 [8192, 64, 576], P('seq', 'head'), may hold values from -10 to 10
- cache: bfloat16 [32768, 576], P('seq'), may hold values from -6 to 6
- grad_out: bfloat16 [8192, 64, 128], P('seq', 'head'), may hold values from -6 to 6
- value_weight: bfloat16 [64, 512, 128], P('head'), may hold values from -0.25 to 0.25
- picked: int32 [256, 4], P('seq'), may hold values from 0 to 255, as said below
Outputs:
- d_query: bfloat16 [8192, 64, 576], P('seq', 'head')
- d_cache: float32 [256, 128, 576], P('seq', 'head')
- d_value_weight: bfloat16 [64, 512, 128], P('head')
The draws below stay inside these ranges and needn't reach their ends.
Inputs may be any that keep to these rules, and one draw needn't show every extreme that they name: `picked`: row g names 4 different blocks, each starting at or before the first query of block g. One of them is the block that holds query block g; every other one ends before position 24576. The rows of one index of seq together name at most 1 different blocks of any one owner (owner o holds blocks o * 4 to o * 4 + 3), and in every draw some owner has exactly 1 of its blocks named by every index of seq.
All inputs are finite; a program needn't handle non-finite values.
Results may differ from the reference program's by a relative error of at most 0.01.
Values may be sent and summed in bfloat16 or wider, within the bound.
No kernel may reach another device: no remote copies, remote signals or barrier semaphores. Data moves between devices by JAX's collectives and lax.ppermute only.
A program may use at most 128 MiB of HBM per device.

```python
import jax
import jax.numpy as jnp
from jax import lax

HEADS = 64
KVL = 512
ROPE = 64
VD = 128
BLOCK = 128
QB = 32
TOPB = 4
Q_DEV = 128
QUERIES = 8192
CTX = 32768
QBLOCKS = 256
NBLK_DEV = 4
CAP = 1
FULL = 48


def distinct_order(key, array_shape):
    length = array_shape[-1]
    scores = jax.random.randint(key, array_shape, 0, 1 << 16)
    scores = scores * length + jnp.arange(length, dtype=jnp.int32)
    return jnp.argsort(scores, axis=-1).astype(jnp.int32)


def draw_cache(key, part):
    array_shape = (CTX, KVL + ROPE)
    drawn = jnp.clip(jax.random.normal(jax.random.fold_in(key, 1), array_shape, jnp.float32), -6.0, 6.0)
    return drawn.astype(jnp.bfloat16)


def draw_query(key, part):
    array_shape = (QUERIES, HEADS, KVL + ROPE)
    drawn = jnp.clip(jax.random.normal(jax.random.fold_in(key, 2), array_shape, jnp.float32), -6.0, 6.0)
    return drawn.astype(jnp.bfloat16)


def draw_picked(key, part):
    per_device = Q_DEV // QB
    seq_count = QUERIES // Q_DEV
    candidates_per = FULL * CAP
    local_order = distinct_order(jax.random.fold_in(key, 11), (seq_count, FULL, NBLK_DEV))
    owner_ids = jnp.arange(FULL, dtype=jnp.int32)
    candidates = owner_ids[None, :, None] * NBLK_DEV + local_order[:, :, :CAP]
    hot_owner = jax.random.randint(jax.random.fold_in(key, 12), (), 0, FULL)
    hot_blocks = jnp.take(candidates, hot_owner, axis=1)
    flat_candidates = candidates.reshape(seq_count, candidates_per)
    is_hot = (jnp.arange(candidates_per, dtype=jnp.int32) // CAP == hot_owner).astype(jnp.int32)
    scores = jax.random.randint(jax.random.fold_in(key, 13), (seq_count, per_device, candidates_per), 0, 1 << 16)
    scores = scores * candidates_per + jnp.arange(candidates_per, dtype=jnp.int32) + is_hot * (1 << 28)
    ranking = jnp.argsort(scores, axis=-1)[:, :, :TOPB - 1 - CAP]
    others = jnp.take_along_axis(jnp.broadcast_to(flat_candidates[:, None, :], scores.shape), ranking, axis=-1)
    block_rows = jnp.arange(QBLOCKS, dtype=jnp.int32).reshape(seq_count, per_device)
    own_block = (CTX - QUERIES + block_rows * QB + QB - 1) // BLOCK
    picked_lists = jnp.concatenate([own_block[:, :, None], jnp.broadcast_to(hot_blocks[:, None, :], (seq_count, per_device, CAP)), others], axis=-1)
    placing = distinct_order(jax.random.fold_in(key, 14), (seq_count, per_device, TOPB))
    picked_lists = jnp.take_along_axis(picked_lists, placing, axis=-1)
    return picked_lists.reshape(QBLOCKS, TOPB).astype(jnp.int32)


def levels(key, shape, split, low, high):
    def one(dim, blocks):
        steps = jax.random.uniform(jax.random.fold_in(jax.random.fold_in(key, 6), dim), (blocks,), jnp.float32, low / len(split), high / len(split))
        return jnp.repeat(jnp.exp(steps), shape[dim] // blocks).reshape((-1,) + (1,) * (len(shape) - dim - 1))

    level = one(*split[0])
    for cut in split[1:]:
        level = level * one(*cut)
    return level


def noise(stream_key, shape, deviation, limit, cuts=(), held_as=jnp.bfloat16):
    level = levels(stream_key, shape, cuts, -0.22, 0.18) if cuts else 1.0
    values = jax.random.normal(stream_key, shape, jnp.float32) * deviation * level
    return jnp.minimum(jnp.maximum(values, -limit), limit).astype(held_as)


def setup_inputs(seed: int = 0) -> dict:
    key_of = jax.random.split(jax.random.key(seed), 6)
    return {
        "query": draw_query(jax.random.fold_in(key_of[5], 71), 0),
        "cache": draw_cache(jax.random.fold_in(key_of[5], 71), 0),
        "grad_out": noise(key_of[2], (QUERIES, HEADS, VD), 1.0, 6.0, ((0, 64), (1, 4))),
        "value_weight": noise(key_of[3], (HEADS, KVL, VD), KVL ** -0.5, 0.25, ((0, 4),)),
        "picked": draw_picked(jax.random.fold_in(key_of[5], 71), 0),
    }


SCORE_SCALE = 0.07216878364870323
MASKED = -1.0e30


def block_backward(q_rows, key_rows, d_latent, visible):
    value_rows = key_rows[:, :KVL]
    scores = lax.dot_general(q_rows, key_rows, (((1,), (1,)), ((), ())), preferred_element_type=jnp.float32) * SCORE_SCALE
    scores = jnp.where(visible, scores, MASKED)
    row_max = jnp.max(scores, axis=1, keepdims=True)
    exp_scores = jnp.exp(scores - row_max)
    weights = exp_scores / jnp.sum(exp_scores, axis=1, keepdims=True)
    weights_low = weights.astype(jnp.bfloat16)
    latent_out = jnp.dot(weights_low, value_rows, preferred_element_type=jnp.float32).astype(jnp.bfloat16)
    row_delta = jnp.sum(d_latent.astype(jnp.float32) * latent_out.astype(jnp.float32), axis=1, keepdims=True)
    d_probs = lax.dot_general(d_latent, value_rows, (((1,), (1,)), ((), ())), preferred_element_type=jnp.float32)
    d_scores = (SCORE_SCALE * weights * (d_probs - row_delta)).astype(jnp.bfloat16)
    d_query = jnp.dot(d_scores, key_rows, preferred_element_type=jnp.float32).astype(jnp.bfloat16)
    d_keys = lax.dot_general(d_scores, q_rows, (((0,), (0,)), ((), ())), preferred_element_type=jnp.float32)
    d_values = lax.dot_general(weights_low, d_latent, (((0,), (0,)), ((), ())), preferred_element_type=jnp.float32)
    d_keys = jnp.concatenate([d_keys[:, :KVL] + d_values, d_keys[:, KVL:]], axis=1)
    return d_query, d_keys, latent_out


def reference(query, cache, grad_out, value_weight, picked):
    head_count = query.shape[1]
    row_width = query.shape[2]
    row_count = QB * head_count
    cache_blocks = cache.reshape(CTX // BLOCK, BLOCK, row_width)
    first_pos = CTX - QUERIES
    weight_f = value_weight.astype(jnp.float32)

    def one_block(totals, inputs):
        cache_total, weight_total = totals
        q_block, grad_block, chosen, block_index = inputs
        d_latent = jnp.einsum("qhv,hcv->qhc", grad_block.astype(jnp.float32), weight_f).astype(jnp.bfloat16)
        key_rows = jnp.take(cache_blocks, chosen, axis=0).reshape(TOPB * BLOCK, row_width)
        query_pos = first_pos + block_index * QB + jnp.arange(QB, dtype=jnp.int32)
        row_pos = jnp.repeat(query_pos, head_count)
        key_pos = (chosen[:, None] * BLOCK + jnp.arange(BLOCK, dtype=jnp.int32)[None, :]).reshape(TOPB * BLOCK)
        visible = key_pos[None, :] <= row_pos[:, None]
        d_query, d_keys, latent_out = block_backward(q_block.reshape(row_count, row_width), key_rows, d_latent.reshape(row_count, KVL), visible)
        cache_total = cache_total.at[chosen].add(d_keys.reshape(TOPB, BLOCK, row_width))
        weight_total = weight_total + jnp.einsum("qhc,qhv->hcv", latent_out.reshape(QB, head_count, KVL).astype(jnp.float32), grad_block.astype(jnp.float32))
        return (cache_total, weight_total), d_query.reshape(QB, head_count, row_width)

    start_totals = (jnp.zeros((CTX // BLOCK, BLOCK, row_width), jnp.float32), jnp.zeros((head_count, KVL, VD), jnp.float32))
    inputs = (query.reshape(QBLOCKS, QB, head_count, row_width), grad_out.reshape(QBLOCKS, QB, head_count, VD), picked, jnp.arange(QBLOCKS, dtype=jnp.int32))
    (cache_total, weight_total), d_query = lax.scan(one_block, start_totals, inputs)
    return d_query.reshape(QUERIES, head_count, row_width), cache_total, weight_total.astype(jnp.bfloat16)
```

```python
import functools

import jax
import jax.numpy as jnp
from jax import lax
from jax.experimental import pallas as pl
from jax.experimental.pallas import tpu as pltpu
from jax.sharding import PartitionSpec as P

KVL = 512
BLOCK = 128
QB = 32
TOPB = 4
OTHERS = TOPB - 1

SCORE_SCALE = 0.07216878364870323
MASKED = -1e30

Z, Y, C = 8, 4, 2
X = 4
Z_FULL = 6
FIRST_OWN_OWNER = Z_FULL * Y * C


F32 = jnp.float32
BF16 = jnp.bfloat16


def seq_of(z, y, c):
    return ((z % Z) * Y + y % Y) * C + c


def shift_z(array, step, keep=lambda z: True):
    pairs = [
        (seq_of(z, y, c), seq_of(z + step, y, c))
        for z in range(Z)
        for y in range(Y)
        for c in range(C)
        if keep(z)
    ]
    return lax.ppermute(array, "seq", pairs)


def shift_y(array, step):
    pairs = [
        (seq_of(z, y, c), seq_of(z, y + step, c))
        for z in range(Z)
        for y in range(Y)
        for c in range(C)
    ]
    return lax.ppermute(array, "seq", pairs)


def swap_core(array):
    return lax.ppermute(array, "seq", [(s, s ^ 1) for s in range(Z * Y * C)])


def shift_x(array, step):
    return lax.ppermute(array, "head", [(x, (x + step) % X) for x in range(X)])


def gather_z(own, limit=Z):
    right, left = [own], [own]
    for hop in range(4):
        right.append(shift_z(right[-1], 1, lambda z: (z - hop) % Z < limit))
        if hop < 3:
            left.append(shift_z(left[-1], -1, lambda z: (z + hop) % Z < limit))
    return [own, left[1], left[2], left[3], right[4], right[3], right[2], right[1]]


def gather_y(own):
    half = own.shape[0] // 2
    right = shift_y(own, 1)
    left = shift_y(own, -1)
    far = [shift_y(right[:half], 1), shift_y(left[half:], -1)]
    return [own, left, jnp.concatenate(far), right]


def reduce_z(terms, narrow, limit=Z):
    right, left = narrow(terms[4]), narrow(terms[5])
    for hop in range(4):
        arrived = shift_z(right, 1, lambda z: (z + 4 - hop) % Z < limit).astype(F32)
        right = narrow(arrived + terms[3 - hop].astype(F32)) if hop < 3 else arrived
    for hop in range(3):
        arrived = shift_z(left, -1, lambda z: (z - 3 + hop) % Z < limit).astype(F32)
        left = narrow(arrived + terms[6 + hop].astype(F32)) if hop < 2 else arrived
    return terms[0].astype(F32) + right + left


def reduce_y(terms, narrow):
    half = terms[0].shape[0] // 2
    far_right = shift_y(narrow(terms[2][:half]), 1).astype(F32)
    far_left = shift_y(narrow(terms[2][half:]), -1).astype(F32)
    right_low = shift_y(narrow(terms[1][:half].astype(F32) + far_right), 1)
    right_high = shift_y(narrow(terms[1][half:]), 1)
    left_low = shift_y(narrow(terms[3][:half]), -1)
    left_high = shift_y(narrow(terms[3][half:].astype(F32) + far_left), -1)
    low = terms[0][:half].astype(F32) + right_low.astype(F32) + left_low.astype(F32)
    high = terms[0][half:].astype(F32) + right_high.astype(F32) + left_high.astype(F32)
    return jnp.concatenate([low, high])


def attend_kernel(x_ref, q_ref, dl_ref, other_ref, own_ref, dq_ref, lat_ref, dk_ref, keys, own_sum):
    block = pl.program_id(0)
    rows, width = q_ref.shape
    heads = rows // QB
    quarter = other_ref.shape[2]
    n_other = X * OTHERS * quarter
    keys[:n_other] = other_ref[...].reshape(n_other, width)
    keys[n_other:] = own_ref[...].reshape(X * quarter, width)
    q = q_ref[...]
    dl = dl_ref[...]
    k = keys[...]
    v = keys[:, :KVL]
    n_keys = k.shape[0]
    scores = lax.dot_general(q, k, (((1,), (1,)), ((), ())), preferred_element_type=F32)
    scores = scores * SCORE_SCALE
    col = lax.broadcasted_iota(jnp.int32, (rows, n_keys - n_other), 1)
    row = lax.broadcasted_iota(jnp.int32, (rows, n_keys - n_other), 0)
    source = (x_ref[0] + X - col // quarter) % X
    visible = source * quarter + col % quarter <= block * QB + row // heads
    scores = jnp.concatenate(
        [scores[:, :n_other], jnp.where(visible, scores[:, n_other:], MASKED)], axis=1
    )
    row_max = jnp.max(scores, axis=1, keepdims=True)
    exp_scores = jnp.exp(scores - row_max)
    weights = exp_scores / jnp.sum(exp_scores, axis=1, keepdims=True)
    weights_low = weights.astype(BF16)
    latent = jnp.dot(weights_low, v, preferred_element_type=F32).astype(BF16)
    lat_ref[...] = latent
    delta = jnp.sum(dl.astype(F32) * latent.astype(F32), axis=1, keepdims=True)
    d_probs = lax.dot_general(dl, v, (((1,), (1,)), ((), ())), preferred_element_type=F32)
    d_scores = (SCORE_SCALE * weights * (d_probs - delta)).astype(BF16)
    dq_ref[...] = jnp.dot(d_scores, k, preferred_element_type=F32).astype(BF16)
    d_keys = lax.dot_general(d_scores, q, (((0,), (0,)), ((), ())), preferred_element_type=F32)
    d_values = lax.dot_general(
        weights_low, dl, (((0,), (0,)), ((), ())), preferred_element_type=F32
    )
    d_keys = jnp.concatenate([d_keys[:, :KVL] + d_values, d_keys[:, KVL:]], axis=1)
    dk_ref[:, pl.ds(OTHERS * block, OTHERS)] = (
        d_keys[:n_other].astype(BF16).reshape(X, OTHERS, quarter, width)
    )
    d_own = d_keys[n_other:]

    @pl.when(block == 0)
    def _():
        own_sum[...] = d_own

    @pl.when(block > 0)
    def _():
        own_sum[...] += d_own

    @pl.when(block == pl.num_programs(0) - 1)
    def _():
        total = own_sum[...].astype(BF16).reshape(X, 1, quarter, width)
        dk_ref[:, dk_ref.shape[1] - 1 :] = total


def attend(x, q, dl, keys, interpret=False):
    rows, width = q.shape
    _, slots, quarter, _ = keys.shape
    blocks = (slots - 1) // OTHERS
    per = rows // blocks
    n_keys = TOPB * X * quarter
    return pl.pallas_call(
        attend_kernel,
        grid_spec=pltpu.PrefetchScalarGridSpec(
            num_scalar_prefetch=1,
            grid=(blocks,),
            in_specs=[
                pl.BlockSpec((per, width), lambda g, x: (g, 0)),
                pl.BlockSpec((per, KVL), lambda g, x: (g, 0)),
                pl.BlockSpec((X, OTHERS, quarter, width), lambda g, x: (0, g, 0, 0)),
                pl.BlockSpec((X, 1, quarter, width), lambda g, x: (0, slots - 1, 0, 0)),
            ],
            out_specs=[
                pl.BlockSpec((per, width), lambda g, x: (g, 0)),
                pl.BlockSpec((per, KVL), lambda g, x: (g, 0)),
                pl.BlockSpec((X, slots, quarter, width), lambda g, x: (0, 0, 0, 0)),
            ],
            scratch_shapes=[
                pltpu.VMEM((n_keys, width), BF16),
                pltpu.VMEM((X * quarter, width), F32),
            ],
        ),
        out_shape=[
            jax.ShapeDtypeStruct((rows, width), BF16),
            jax.ShapeDtypeStruct((rows, KVL), BF16),
            jax.ShapeDtypeStruct((X, slots, quarter, width), BF16),
        ],
        interpret=interpret,
        compiler_params=pltpu.CompilerParams(vmem_limit_bytes=56 * 2**20),
        name="attend",
    )(x.reshape(1), q, dl, keys, keys)


def spread_kernel(at_a_ref, at_b_ref, mine_ref, theirs_ref, a_ref, b_ref, sum_a, sum_b):
    half = a_ref.shape[1]
    sum_a[...] = jnp.zeros_like(sum_a)
    sum_b[...] = jnp.zeros_like(sum_b)
    count = mine_ref.shape[0]
    for slot in range(2 * count):
        share = (mine_ref[slot] if slot < count else theirs_ref[slot - count]).astype(F32)
        a, b = at_a_ref[slot], at_b_ref[slot]
        sum_a[a] += share[:half]
        sum_b[b] += share[half:]
    a_ref[...] = sum_a[: a_ref.shape[0]].astype(BF16)
    b_ref[...] = sum_b[: b_ref.shape[0]].astype(BF16)


def spread(at_a, at_b, mine, theirs, blocks, interpret=False):
    _, quarter, width = mine.shape
    half = quarter // 2
    shape = jax.ShapeDtypeStruct((blocks, half, width), BF16)
    vmem = pl.BlockSpec(memory_space=pltpu.VMEM)
    smem = pl.BlockSpec(memory_space=pltpu.SMEM)
    return pl.pallas_call(
        spread_kernel,
        in_specs=[smem, smem, vmem, vmem],
        out_specs=[vmem, vmem],
        out_shape=[shape, shape],
        scratch_shapes=[pltpu.VMEM((blocks + 1, half, width), F32)] * 2,
        interpret=interpret,
        compiler_params=pltpu.CompilerParams(vmem_limit_bytes=40 * 2**20),
        name="spread",
    )(at_a, at_b, mine, theirs)


def local(query, cache, grad_out, value_weight, picked):
    q_dev, heads_here, width = query.shape
    block_count = cache.shape[0] // BLOCK
    seq = lax.axis_index("seq")
    x = lax.axis_index("head")
    z, y, c = seq // (Y * C), seq // C % Y, seq % C
    quarter = BLOCK // X
    half = quarter // 2
    g_here = q_dev // QB
    others = g_here * OTHERS
    rows = q_dev * heads_here

    part = lax.dynamic_slice_in_dim(
        cache.reshape(block_count, BLOCK, width), x * quarter, quarter, 1
    )

    own_id = FIRST_OWN_OWNER * block_count + seq
    is_other = picked != own_id
    rank = jnp.cumsum(is_other.astype(jnp.int32), axis=1) - 1
    at_rank = is_other[:, :, None] & (rank[:, :, None] == jnp.arange(OTHERS, dtype=jnp.int32))
    my_ids = jnp.sum(jnp.where(at_rank, picked[:, :, None], 0), axis=1).reshape(others)
    their_ids = swap_core(my_ids)
    ids = jnp.concatenate([my_ids, their_ids])
    owner, block = ids // block_count, ids % block_count
    here = owner % C == c
    z_off = (owner // (Y * C) - z) % Z
    y_off = (owner // C % Y - y) % Y
    at_a = (y_off * Z + z_off) * block_count + block
    at_b = (z_off * Y + y_off) * block_count + block
    all_blocks = Z * Y * block_count

    piece_a = jnp.stack(gather_z(part[:, :half], Z_FULL))
    piece_b = jnp.stack(gather_y(part[:, half:]))
    all_a = jnp.stack(gather_y(piece_a)).reshape(all_blocks, half, width)
    all_b = jnp.stack(gather_z(piece_b, Z_FULL)).reshape(all_blocks, half, width)
    own_part = sum(
        lax.ppermute(
            part[j],
            "seq",
            [(o, (o - FIRST_OWN_OWNER) * block_count + j) for o in range(FIRST_OWN_OWNER, Z * Y * C)],
        )
        for j in range(block_count)
    )
    taken = jnp.concatenate(
        [jnp.take(all_a, at_a, axis=0), jnp.take(all_b, at_b, axis=0)], axis=1
    )
    arrived = swap_core(taken[others:])
    slots = jnp.where(here[:others, None, None], taken[:others], arrived)
    slots = jnp.concatenate([slots, own_part[None]])

    low = (others + 1 + 1) // 2
    from_left = shift_x(slots, 1)
    from_right = shift_x(slots, -1)
    far = jnp.concatenate([shift_x(from_left[:low], 1), shift_x(from_right[low:], -1)])
    keys = jnp.stack([slots, from_left, far, from_right])

    d_latent = jnp.einsum(
        "qhv,hcv->qhc", grad_out, value_weight, preferred_element_type=F32
    ).astype(BF16)
    d_query, latent_out, d_keys = attend(
        x, query.reshape(rows, width), d_latent.reshape(rows, KVL), keys
    )

    narrow = lambda array: array.astype(BF16)
    wide = lambda array: array.astype(F32)
    low_far = shift_x(d_keys[2, :low], -1)
    high_far = shift_x(d_keys[2, low:], 1)
    high_left = shift_x(d_keys[1, low:], -1)
    low_right = shift_x(d_keys[3, :low], 1)
    low_left = shift_x(narrow(wide(low_far) + wide(d_keys[1, :low])), -1)
    high_right = shift_x(narrow(wide(high_far) + wide(d_keys[3, low:])), 1)
    shares = jnp.concatenate(
        [
            wide(d_keys[0, :low]) + wide(low_left) + wide(low_right),
            wide(d_keys[0, low:]) + wide(high_left) + wide(high_right),
        ]
    )
    shares_low = narrow(shares)
    their_shares = swap_core(shares_low[:others])
    dump = jnp.int32(all_blocks)
    sum_a, sum_b = spread(
        jnp.where(here, at_a, dump),
        jnp.where(here, at_b, dump),
        shares_low[:others],
        their_shares,
        all_blocks,
    )
    sum_a = sum_a.reshape(Y, Z, block_count, half, width)
    sum_b = sum_b.reshape(Z, Y, block_count, half, width)
    mine_a = reduce_z(reduce_y(sum_a, narrow), narrow, Z_FULL)
    mine_b = reduce_y(reduce_z(sum_b, narrow, Z_FULL), narrow)
    own_share = shares_low[others]
    own_back = jnp.stack(
        [
            lax.ppermute(
                own_share,
                "seq",
                [
                    ((o - FIRST_OWN_OWNER) * block_count + j, o)
                    for o in range(FIRST_OWN_OWNER, Z * Y * C)
                ],
            )
            for j in range(block_count)
        ]
    )
    d_cache = jnp.concatenate([mine_a, mine_b], axis=1) + wide(own_back)

    terms = jnp.einsum(
        "qhc,qhv->hcv",
        latent_out.reshape(q_dev, heads_here, KVL),
        grad_out,
        preferred_element_type=F32,
    )
    v_dim = terms.shape[-1]
    terms = terms.reshape(C, Z, Y, -1, v_dim)
    same = lambda array: array
    kept = lax.dynamic_index_in_dim(terms, c, 0, keepdims=False)
    sent = lax.dynamic_index_in_dim(terms, 1 - c, 0, keepdims=False)
    kept = kept + swap_core(sent)
    z_order = (z + jnp.arange(Z, dtype=jnp.int32)) % Z
    y_order = (y + jnp.arange(Y, dtype=jnp.int32)) % Y
    order = (z_order[:, None] * Y + y_order[None, :]).reshape(Z * Y)
    kept = jnp.take(kept.reshape(Z * Y, -1, v_dim), order, axis=0).reshape(Z, Y, -1, v_dim)
    mine = narrow(reduce_y(reduce_z(kept, same), same))
    both = lax.dynamic_update_index_in_dim(
        lax.dynamic_update_index_in_dim(jnp.zeros((C, *mine.shape), BF16), mine, c, 0),
        swap_core(mine),
        1 - c,
        0,
    )
    columns = jnp.stack(gather_y(both.reshape(-1, v_dim)))
    whole = jnp.stack(gather_z(columns)).reshape(Z * Y, C, -1, v_dim)
    z_back = (jnp.arange(Z, dtype=jnp.int32) - z) % Z
    y_back = (jnp.arange(Y, dtype=jnp.int32) - y) % Y
    back = (z_back[:, None] * Y + y_back[None, :]).reshape(Z * Y)
    whole = jnp.moveaxis(jnp.take(whole, back, axis=0), 1, 0)
    d_value_weight = whole.reshape(value_weight.shape)
    return d_query.reshape(query.shape), d_cache, d_value_weight


def solution(mesh):
    in_specs = (
        P("seq", "head", None),
        P("seq", None),
        P("seq", "head", None),
        P("head", None, None),
        P("seq", None),
    )
    out_specs = (P("seq", "head", None), P("seq", "head", None), P("head", None, None))
    return jax.shard_map(local, mesh=mesh, in_specs=in_specs, out_specs=out_specs, check_vma=False)
```

```python
import jax
import jax.numpy as jnp
from jax import lax
from jax.experimental import pallas as pl
from jax.experimental.pallas import tpu as pltpu
from jax.sharding import PartitionSpec as P

KVL = 512
BLOCK = 128
QB = 32
TOPB = 4
OTHERS = TOPB - 1

SCORE_SCALE = 0.07216878364870323
MASKED = -1e30

Z, Y, C = 8, 4, 2
X = 4
Z_FULL = 6
FIRST_OWN_OWNER = Z_FULL * Y * C


F32 = jnp.float32
BF16 = jnp.bfloat16


def seq_of(z, y, c):
    return ((z % Z) * Y + y % Y) * C + c


def shift_z(array, step, sends=lambda z: True):
    pairs = [
        (seq_of(z, y, c), seq_of(z + step, y, c))
        for z in range(Z)
        for y in range(Y)
        for c in range(C)
        if sends(z)
    ]
    return lax.ppermute(array, "seq", pairs)


def shift_x(array, step):
    return lax.ppermute(array, "head", [(x, (x + step) % X) for x in range(X)])


def trade_yc(blocks):
    groups = [[seq_of(z, 0, 0) + i for i in range(Y * C)] for z in range(Z)]
    return lax.all_to_all(
        blocks, "seq", split_axis=0, concat_axis=0, axis_index_groups=groups, tiled=True
    )


def trade_z(blocks):
    groups = [[seq_of(z, 0, 0) + i for z in range(Z)] for i in range(Y * C)]
    return lax.all_to_all(
        blocks, "seq", split_axis=0, concat_axis=0, axis_index_groups=groups, tiled=True
    )


def narrow(array):
    return array.astype(BF16)


def wide(array):
    return array.astype(F32)


def attend_kernel(x_ref, q_ref, dl_ref, *refs):
    low_refs, own_refs, high_refs = refs[:X], refs[X : 2 * X], refs[2 * X : 3 * X]
    dq_ref, lat_ref = refs[3 * X : 3 * X + 2]
    d_low_refs, d_high_refs = refs[3 * X + 2 : 4 * X + 2], refs[4 * X + 2 : 5 * X + 2]
    keys, own_sum = refs[5 * X + 2 :]
    block = pl.program_id(0)
    half_blocks = pl.num_programs(0) // 2
    rows, width = q_ref.shape
    heads = rows // QB
    quarter = own_refs[0].shape[1]
    n_part = OTHERS * quarter
    n_other = X * n_part

    @pl.when(block < half_blocks)
    def _():
        for j in range(X):
            keys[j * n_part : (j + 1) * n_part] = low_refs[j][...].reshape(n_part, width)

    @pl.when(block >= half_blocks)
    def _():
        for j in range(X):
            keys[j * n_part : (j + 1) * n_part] = high_refs[j][...].reshape(n_part, width)

    @pl.when(block == 0)
    def _():
        for j in range(X):
            keys[n_other + j * quarter : n_other + (j + 1) * quarter] = own_refs[j][0]

    q = q_ref[...]
    dl = dl_ref[...]
    k = keys[...]
    v = keys[:, :KVL]
    n_keys = k.shape[0]
    scores = lax.dot_general(q, k, (((1,), (1,)), ((), ())), preferred_element_type=F32)
    scores = scores * SCORE_SCALE
    col = lax.broadcasted_iota(jnp.int32, (rows, n_keys - n_other), 1)
    row = lax.broadcasted_iota(jnp.int32, (rows, n_keys - n_other), 0)
    source = (x_ref[0] + X - col // quarter) % X
    visible = source * quarter + col % quarter <= block * QB + row // heads
    scores = jnp.concatenate(
        [scores[:, :n_other], jnp.where(visible, scores[:, n_other:], MASKED)], axis=1
    )
    row_max = jnp.max(scores, axis=1, keepdims=True)
    exp_scores = jnp.exp(scores - row_max)
    weights = exp_scores / jnp.sum(exp_scores, axis=1, keepdims=True)
    weights_low = narrow(weights)
    latent = narrow(jnp.dot(weights_low, v, preferred_element_type=F32))
    lat_ref[...] = latent
    delta = jnp.sum(wide(dl) * wide(latent), axis=1, keepdims=True)
    d_probs = lax.dot_general(dl, v, (((1,), (1,)), ((), ())), preferred_element_type=F32)
    d_scores = narrow(SCORE_SCALE * weights * (d_probs - delta))
    dq_ref[...] = narrow(jnp.dot(d_scores, k, preferred_element_type=F32))
    d_keys = lax.dot_general(d_scores, q, (((0,), (0,)), ((), ())), preferred_element_type=F32)
    d_values = lax.dot_general(
        weights_low, dl, (((0,), (0,)), ((), ())), preferred_element_type=F32
    )
    d_keys = jnp.concatenate([d_keys[:, :KVL] + d_values, d_keys[:, KVL:]], axis=1)
    d_other = narrow(d_keys[:n_other]).reshape(X, OTHERS, quarter, width)

    @pl.when(block < half_blocks)
    def _():
        for j in range(X):
            d_low_refs[j][pl.ds(OTHERS * block, OTHERS)] = d_other[j]

    @pl.when(block >= half_blocks)
    def _():
        for j in range(X):
            d_high_refs[j][pl.ds(OTHERS * (block - half_blocks), OTHERS)] = d_other[j]

    d_own = d_keys[n_other:]

    @pl.when(block == 0)
    def _():
        own_sum[...] = d_own

    @pl.when(block > 0)
    def _():
        own_sum[...] += d_own

    @pl.when(block == pl.num_programs(0) - 1)
    def _():
        last = d_low_refs[0].shape[0] - 1
        for j in range(X):
            d_low_refs[j][last] = narrow(own_sum[j * quarter : (j + 1) * quarter])


def attend(x, q, dl, low, high, interpret=False):
    rows, width = q.shape
    n_low, quarter, _ = low[0].shape
    n_high = high[0].shape[0]
    blocks = (n_low - 1 + n_high) // OTHERS
    half = blocks // 2
    per = rows // blocks
    n_keys = TOPB * X * quarter
    part = (OTHERS, quarter, width)
    return pl.pallas_call(
        attend_kernel,
        grid_spec=pltpu.PrefetchScalarGridSpec(
            num_scalar_prefetch=1,
            grid=(blocks,),
            in_specs=[
                pl.BlockSpec((per, width), lambda g, x: (g, 0)),
                pl.BlockSpec((per, KVL), lambda g, x: (g, 0)),
            ]
            + [pl.BlockSpec(part, lambda g, x: (jnp.minimum(g, half - 1), 0, 0))] * X
            + [pl.BlockSpec((1, quarter, width), lambda g, x: (n_low - 1, 0, 0))] * X
            + [pl.BlockSpec(part, lambda g, x: (jnp.maximum(g - half, 0), 0, 0))] * X,
            out_specs=[
                pl.BlockSpec((per, width), lambda g, x: (g, 0)),
                pl.BlockSpec((per, KVL), lambda g, x: (g, 0)),
            ]
            + [pl.BlockSpec((n_low, quarter, width), lambda g, x: (0, 0, 0))] * X
            + [pl.BlockSpec((n_high, quarter, width), lambda g, x: (0, 0, 0))] * X,
            scratch_shapes=[
                pltpu.VMEM((n_keys, width), BF16),
                pltpu.VMEM((X * quarter, width), F32),
            ],
        ),
        out_shape=[
            jax.ShapeDtypeStruct((rows, width), BF16),
            jax.ShapeDtypeStruct((rows, KVL), BF16),
        ]
        + [jax.ShapeDtypeStruct((n_low, quarter, width), BF16)] * X
        + [jax.ShapeDtypeStruct((n_high, quarter, width), BF16)] * X,
        interpret=interpret,
        compiler_params=pltpu.CompilerParams(vmem_limit_bytes=56 * 2**20),
        name="attend",
    )(x.reshape(1), q, dl, *low, *low, *high)


def send_back_kernel(at_ref, *refs):
    low_refs, high_refs = refs[:3], refs[3:6]
    out_ref, own_ref, total = refs[6:]
    n_low, n_high = low_refs[0].shape[0], high_refs[0].shape[0]
    total[...] = jnp.zeros_like(total)
    for slot in range(n_low + n_high - 1):
        refs_here, index = (low_refs, slot) if slot < n_low - 1 else (high_refs, slot - n_low + 1)
        share = wide(refs_here[0][index]) + wide(refs_here[1][index]) + wide(refs_here[2][index])
        total[at_ref[slot]] += share
    last = n_low - 1
    own_ref[...] = narrow(
        wide(low_refs[0][last]) + wide(low_refs[1][last]) + wide(low_refs[2][last])
    )
    out_ref[...] = narrow(total[...])


def send_back(at, low, high, places, interpret=False):
    _, quarter, width = low[0].shape
    vmem = pl.BlockSpec(memory_space=pltpu.VMEM)
    return pl.pallas_call(
        send_back_kernel,
        in_specs=[pl.BlockSpec(memory_space=pltpu.SMEM)] + [vmem] * 6,
        out_specs=[vmem, vmem],
        out_shape=[
            jax.ShapeDtypeStruct((places, quarter, width), BF16),
            jax.ShapeDtypeStruct((quarter, width), BF16),
        ],
        scratch_shapes=[pltpu.VMEM((places, quarter, width), F32)],
        interpret=interpret,
        compiler_params=pltpu.CompilerParams(vmem_limit_bytes=40 * 2**20),
        name="send_back",
    )(at, *low, *high)


def by_owner_kernel(at_ref, in_ref, *refs):
    out_refs, total = refs[:-1], refs[-1]
    total[...] = jnp.zeros_like(total)
    for slot in range(in_ref.shape[0]):
        total[at_ref[slot]] += wide(in_ref[slot])
    blocks = out_refs[0].shape[0]
    for j, out_ref in enumerate(out_refs):
        out_ref[...] = narrow(total[j * blocks : (j + 1) * blocks])


def by_owner(at, received, blocks, interpret=False):
    _, quarter, width = received.shape
    vmem = pl.BlockSpec(memory_space=pltpu.VMEM)
    return pl.pallas_call(
        by_owner_kernel,
        in_specs=[pl.BlockSpec(memory_space=pltpu.SMEM), vmem],
        out_specs=[vmem] * Z,
        out_shape=[jax.ShapeDtypeStruct((blocks, quarter, width), BF16)] * Z,
        scratch_shapes=[pltpu.VMEM((Z * blocks + 1, quarter, width), F32)],
        interpret=interpret,
        compiler_params=pltpu.CompilerParams(vmem_limit_bytes=40 * 2**20),
        name="by_owner",
    )(at, received)


def local(query, cache, grad_out, value_weight, picked):
    q_dev, heads_here, width = query.shape
    block_count = cache.shape[0] // BLOCK
    seq = lax.axis_index("seq")
    x = lax.axis_index("head")
    z = seq // (Y * C)
    peers = Y * C
    quarter = BLOCK // X
    g_here = q_dev // QB
    others = g_here * OTHERS
    rows = q_dev * heads_here

    part = lax.dynamic_slice_in_dim(
        cache.reshape(block_count, BLOCK, width), x * quarter, quarter, 1
    )
    steps = (4, -3, 3, -2, 2, -1, 1)
    pieces = [part] + [None] * (Z - 1)
    for step in steps:
        pieces[-step % Z] = shift_z(part, step, lambda z: z < Z_FULL)
    own_part = sum(
        lax.ppermute(
            part[j],
            "seq",
            [(o, (o - FIRST_OWN_OWNER) * block_count + j) for o in range(FIRST_OWN_OWNER, Z * peers)],
        )
        for j in range(block_count)
    )

    own_id = FIRST_OWN_OWNER * block_count + seq
    is_other = picked != own_id
    rank = jnp.cumsum(is_other.astype(jnp.int32), axis=1) - 1
    at_rank = is_other[:, :, None] & (rank[:, :, None] == jnp.arange(OTHERS, dtype=jnp.int32))
    ids = jnp.sum(jnp.where(at_rank, picked[:, :, None], 0), axis=1).reshape(others)
    owner, block = ids // block_count, ids % block_count
    place = owner % peers * Z_FULL + owner // peers
    places = peers * Z_FULL
    asked = place[:, None] == jnp.arange(places, dtype=jnp.int32)[None, :]
    wanted = jnp.max(jnp.where(asked, block[:, None], -1), axis=0)
    asked_here = trade_yc(wanted.reshape(peers, 1, Z_FULL)).reshape(peers, Z_FULL)
    z_off = (jnp.arange(Z_FULL, dtype=jnp.int32) - z) % Z
    at_piece = (z_off[None, :] * block_count + asked_here).reshape(places)
    valid = (asked_here >= 0).reshape(places)

    along_z = jnp.stack(pieces).reshape(Z * block_count, quarter, width)
    packed = jnp.take(along_z, jnp.where(valid, at_piece, 0), axis=0)
    fetched = trade_yc(packed.reshape(peers, Z_FULL, quarter, width))
    fetched = fetched.reshape(places, quarter, width)
    n_high = others // 2
    low = jnp.concatenate([jnp.take(fetched, place[:n_high], axis=0), own_part[None]])
    high = jnp.take(fetched, place[n_high:], axis=0)

    low_from_left = shift_x(low, 1)
    high_from_right = shift_x(high, -1)
    low_from_right = shift_x(low, -1)
    high_from_left = shift_x(high, 1)
    low_far = shift_x(low_from_left, 1)
    high_far = shift_x(high_from_right, -1)

    d_latent = narrow(
        jnp.einsum("qhv,hcv->qhc", grad_out, value_weight, preferred_element_type=F32)
    )
    d_query, latent_out, *d_keys = attend(
        x,
        query.reshape(rows, width),
        d_latent.reshape(rows, KVL),
        [low, low_from_left, low_far, low_from_right],
        [high, high_from_left, high_far, high_from_right],
    )
    d_low, d_high = d_keys[:X], d_keys[X:]

    terms = jnp.einsum(
        "qhc,qhv->hcv",
        latent_out.reshape(q_dev, heads_here, KVL),
        grad_out,
        preferred_element_type=F32,
    )
    v_dim = terms.shape[-1]
    terms = narrow(terms).reshape(peers, -1, v_dim)
    terms = jnp.sum(wide(trade_yc(terms)), axis=0)
    terms = narrow(terms).reshape(Z, -1, v_dim)
    terms = narrow(jnp.sum(wide(trade_z(terms)), axis=0))
    terms = trade_z(jnp.broadcast_to(terms, (Z, *terms.shape))).reshape(-1, v_dim)
    terms = trade_yc(jnp.broadcast_to(terms, (peers, *terms.shape)))
    d_value_weight = terms.reshape(value_weight.shape)

    low_relay = shift_x(d_low[2], -1)
    high_relay = shift_x(d_high[2], 1)
    high_left = shift_x(d_high[1], -1)
    low_right = shift_x(d_low[3], 1)
    low_left = shift_x(narrow(wide(low_relay) + wide(d_low[1])), -1)
    high_right = shift_x(narrow(wide(high_relay) + wide(d_high[3])), 1)
    back, own_share = send_back(
        place, [d_low[0], low_right, low_left], [d_high[0], high_left, high_right], places
    )
    own_back = jnp.stack(
        [
            lax.ppermute(
                own_share,
                "seq",
                [
                    ((o - FIRST_OWN_OWNER) * block_count + j, o)
                    for o in range(FIRST_OWN_OWNER, Z * peers)
                ],
            )
            for j in range(block_count)
        ]
    )
    received = trade_yc(back.reshape(peers, Z_FULL, quarter, width))
    by_z = by_owner(
        jnp.where(valid, at_piece, Z * block_count),
        received.reshape(places, quarter, width),
        block_count,
    )
    d_cache = wide(by_z[0]) + wide(own_back)
    for step in steps:
        arrived = shift_z(by_z[step % Z], step, lambda z: (z + step) % Z < Z_FULL)
        d_cache = d_cache + wide(arrived)
    return d_query.reshape(query.shape), d_cache, d_value_weight


def solution(mesh):
    in_specs = (
        P("seq", "head", None),
        P("seq", None),
        P("seq", "head", None),
        P("head", None, None),
        P("seq", None),
    )
    out_specs = (P("seq", "head", None), P("seq", "head", None), P("head", None, None))
    return jax.shard_map(local, mesh=mesh, in_specs=in_specs, out_specs=out_specs, check_vma=False)
```

```python
import jax
import jax.numpy as jnp
from jax import lax
from jax.experimental import pallas as pl
from jax.experimental.pallas import tpu as pltpu
from jax.sharding import PartitionSpec as P

KVL = 512
BLOCK = 128
QB = 32
TOPB = 4
OTHERS = TOPB - 1

SCORE_SCALE = 0.07216878364870323
MASKED = -1e30

Z, Y, C = 8, 4, 2
X = 4
Z_FULL = 6
FIRST_OWN_OWNER = Z_FULL * Y * C


F32 = jnp.float32
BF16 = jnp.bfloat16


def seq_of(z, y, c):
    return ((z % Z) * Y + y % Y) * C + c


def shift_z(array, step, sends=lambda z: True):
    pairs = [
        (seq_of(z, y, c), seq_of(z + step, y, c))
        for z in range(Z)
        for y in range(Y)
        for c in range(C)
        if sends(z)
    ]
    return lax.ppermute(array, "seq", pairs)


def shift_y(array, step):
    pairs = [
        (seq_of(z, y, c), seq_of(z, y + step, c))
        for z in range(Z)
        for y in range(Y)
        for c in range(C)
    ]
    return lax.ppermute(array, "seq", pairs)


def swap_core(array):
    return lax.ppermute(array, "seq", [(s, s ^ 1) for s in range(Z * Y * C)])


def shift_x(array, step):
    return lax.ppermute(array, "head", [(x, (x + step) % X) for x in range(X)])


def trade_yc(blocks):
    groups = [[seq_of(z, 0, 0) + i for i in range(Y * C)] for z in range(Z)]
    return lax.all_to_all(
        blocks, "seq", split_axis=0, concat_axis=0, axis_index_groups=groups, tiled=True
    )


def narrow(array):
    return array.astype(BF16)


def wide(array):
    return array.astype(F32)


def pack_kernel(block_ref, z_ref, *refs):
    pieces, out_ref, sem = refs[:Z], refs[Z], refs[Z + 1]
    for j in range(Z):
        owner_z = (z_ref[0] + j) % Z

        @pl.when(owner_z < Z_FULL)
        def _():
            for peer in range(Y * C):
                place = peer * Z_FULL + owner_z
                pltpu.make_async_copy(
                    pieces[j].at[block_ref[place]], out_ref.at[place], sem
                ).start()

    pltpu.make_async_copy(out_ref, out_ref, sem).wait()


def pack(blocks, z, pieces):
    hbm = pl.BlockSpec(memory_space=pltpu.HBM)
    smem = pl.BlockSpec(memory_space=pltpu.SMEM)
    return pl.pallas_call(
        pack_kernel,
        in_specs=[smem, smem] + [hbm] * Z,
        out_specs=hbm,
        out_shape=jax.ShapeDtypeStruct((blocks.shape[0], *pieces[0].shape[1:]), BF16),
        scratch_shapes=[pltpu.SemaphoreType.DMA],
        name="pack",
    )(blocks, z.reshape(1), *pieces)


def pick_kernel(place_ref, own_ref, fetched_ref, *refs):
    owns, (low_ref, high_ref, low_sem, high_sem) = refs[:-4], refs[-4:]
    n_low, n_high = low_ref.shape[0], high_ref.shape[0]
    for j, own in enumerate(owns):

        @pl.when(own_ref[0] == j)
        def _():
            pltpu.make_async_copy(own, low_ref.at[n_low - 1], low_sem).start()

    for slot in range(n_low - 1):
        pltpu.make_async_copy(
            fetched_ref.at[place_ref[slot]], low_ref.at[slot], low_sem
        ).start()
    for slot in range(n_high):
        pltpu.make_async_copy(
            fetched_ref.at[place_ref[n_low - 1 + slot]], high_ref.at[slot], high_sem
        ).start()
    pltpu.make_async_copy(low_ref, low_ref, low_sem).wait()
    pltpu.make_async_copy(high_ref, high_ref, high_sem).wait()


def pick(place, own_index, fetched, owns):
    hbm = pl.BlockSpec(memory_space=pltpu.HBM)
    smem = pl.BlockSpec(memory_space=pltpu.SMEM)
    n_high = place.shape[0] // 2
    n_low = place.shape[0] - n_high + 1
    return pl.pallas_call(
        pick_kernel,
        in_specs=[smem, smem, hbm] + [hbm] * len(owns),
        out_specs=[hbm, hbm],
        out_shape=[
            jax.ShapeDtypeStruct((n_low, *fetched.shape[1:]), BF16),
            jax.ShapeDtypeStruct((n_high, *fetched.shape[1:]), BF16),
        ],
        scratch_shapes=[pltpu.SemaphoreType.DMA] * 2,
        name="pick",
    )(place, own_index.reshape(1), fetched, *owns)


def attend_kernel(x_ref, q_ref, dl_ref, *refs):
    low_refs, own_refs, high_refs = refs[:X], refs[X : 2 * X], refs[2 * X : 3 * X]
    dq_ref, lat_ref = refs[3 * X : 3 * X + 2]
    d_low_refs, d_high_refs = refs[3 * X + 2 : 4 * X + 2], refs[4 * X + 2 : 5 * X + 2]
    keys, own_sum = refs[5 * X + 2 :]
    block = pl.program_id(0)
    half_blocks = pl.num_programs(0) // 2
    rows, width = q_ref.shape
    heads = rows // QB
    quarter = own_refs[0].shape[1]
    n_part = OTHERS * quarter
    n_other = X * n_part

    @pl.when(block < half_blocks)
    def _():
        for j in range(X):
            keys[j * n_part : (j + 1) * n_part] = low_refs[j][...].reshape(n_part, width)

    @pl.when(block >= half_blocks)
    def _():
        for j in range(X):
            keys[j * n_part : (j + 1) * n_part] = high_refs[j][...].reshape(n_part, width)

    @pl.when(block == 0)
    def _():
        for j in range(X):
            keys[n_other + j * quarter : n_other + (j + 1) * quarter] = own_refs[j][0]

    q = q_ref[...]
    dl = dl_ref[...]
    k = keys[...]
    v = keys[:, :KVL]
    n_keys = k.shape[0]
    scores = lax.dot_general(q, k, (((1,), (1,)), ((), ())), preferred_element_type=F32)
    scores = scores * SCORE_SCALE
    col = lax.broadcasted_iota(jnp.int32, (rows, n_keys - n_other), 1)
    row = lax.broadcasted_iota(jnp.int32, (rows, n_keys - n_other), 0)
    source = (x_ref[0] + X - col // quarter) % X
    visible = source * quarter + col % quarter <= block * QB + row // heads
    scores = jnp.concatenate(
        [scores[:, :n_other], jnp.where(visible, scores[:, n_other:], MASKED)], axis=1
    )
    row_max = jnp.max(scores, axis=1, keepdims=True)
    exp_scores = jnp.exp(scores - row_max)
    weights = exp_scores / jnp.sum(exp_scores, axis=1, keepdims=True)
    weights_low = narrow(weights)
    latent = narrow(jnp.dot(weights_low, v, preferred_element_type=F32))
    lat_ref[...] = latent
    delta = jnp.sum(wide(dl) * wide(latent), axis=1, keepdims=True)
    d_probs = lax.dot_general(dl, v, (((1,), (1,)), ((), ())), preferred_element_type=F32)
    d_scores = narrow(SCORE_SCALE * weights * (d_probs - delta))
    dq_ref[...] = narrow(jnp.dot(d_scores, k, preferred_element_type=F32))
    d_keys = lax.dot_general(d_scores, q, (((0,), (0,)), ((), ())), preferred_element_type=F32)
    d_values = lax.dot_general(
        weights_low, dl, (((0,), (0,)), ((), ())), preferred_element_type=F32
    )
    d_keys = jnp.concatenate([d_keys[:, :KVL] + d_values, d_keys[:, KVL:]], axis=1)
    d_other = narrow(d_keys[:n_other]).reshape(X, OTHERS, quarter, width)

    @pl.when(block < half_blocks)
    def _():
        for j in range(X):
            d_low_refs[j][pl.ds(OTHERS * block, OTHERS)] = d_other[j]

    @pl.when(block >= half_blocks)
    def _():
        for j in range(X):
            d_high_refs[j][pl.ds(OTHERS * (block - half_blocks), OTHERS)] = d_other[j]

    d_own = d_keys[n_other:]

    @pl.when(block == 0)
    def _():
        own_sum[...] = d_own

    @pl.when(block > 0)
    def _():
        own_sum[...] += d_own

    @pl.when(block == pl.num_programs(0) - 1)
    def _():
        last = d_low_refs[0].shape[0] - 1
        for j in range(X):
            d_low_refs[j][last] = narrow(own_sum[j * quarter : (j + 1) * quarter])


def attend(x, q, dl, low, high, interpret=False):
    rows, width = q.shape
    n_low, quarter, _ = low[0].shape
    n_high = high[0].shape[0]
    blocks = (n_low - 1 + n_high) // OTHERS
    half = blocks // 2
    per = rows // blocks
    n_keys = TOPB * X * quarter
    part = (OTHERS, quarter, width)
    return pl.pallas_call(
        attend_kernel,
        grid_spec=pltpu.PrefetchScalarGridSpec(
            num_scalar_prefetch=1,
            grid=(blocks,),
            in_specs=[
                pl.BlockSpec((per, width), lambda g, x: (g, 0)),
                pl.BlockSpec((per, KVL), lambda g, x: (g, 0)),
            ]
            + [pl.BlockSpec(part, lambda g, x: (jnp.minimum(g, half - 1), 0, 0))] * X
            + [pl.BlockSpec((1, quarter, width), lambda g, x: (n_low - 1, 0, 0))] * X
            + [pl.BlockSpec(part, lambda g, x: (jnp.maximum(g - half, 0), 0, 0))] * X,
            out_specs=[
                pl.BlockSpec((per, width), lambda g, x: (g, 0)),
                pl.BlockSpec((per, KVL), lambda g, x: (g, 0)),
            ]
            + [pl.BlockSpec((n_low, quarter, width), lambda g, x: (0, 0, 0))] * X
            + [pl.BlockSpec((n_high, quarter, width), lambda g, x: (0, 0, 0))] * X,
            scratch_shapes=[
                pltpu.VMEM((n_keys, width), BF16),
                pltpu.VMEM((X * quarter, width), F32),
            ],
        ),
        out_shape=[
            jax.ShapeDtypeStruct((rows, width), BF16),
            jax.ShapeDtypeStruct((rows, KVL), BF16),
        ]
        + [jax.ShapeDtypeStruct((n_low, quarter, width), BF16)] * X
        + [jax.ShapeDtypeStruct((n_high, quarter, width), BF16)] * X,
        interpret=interpret,
        compiler_params=pltpu.CompilerParams(vmem_limit_bytes=56 * 2**20),
        name="attend",
    )(x.reshape(1), q, dl, *low, *low, *high)


def send_back_kernel(at_ref, *refs):
    low_refs, high_refs = refs[:3], refs[3:6]
    out_ref, own_ref, total = refs[6:]
    n_low, n_high = low_refs[0].shape[0], high_refs[0].shape[0]
    total[...] = jnp.zeros_like(total)
    for slot in range(n_low + n_high - 1):
        refs_here, index = (low_refs, slot) if slot < n_low - 1 else (high_refs, slot - n_low + 1)
        share = wide(refs_here[0][index]) + wide(refs_here[1][index]) + wide(refs_here[2][index])
        total[at_ref[slot]] += share
    last = n_low - 1
    own_ref[...] = narrow(
        wide(low_refs[0][last]) + wide(low_refs[1][last]) + wide(low_refs[2][last])
    )
    out_ref[...] = narrow(total[...])


def send_back(at, low, high, places, interpret=False):
    _, quarter, width = low[0].shape
    vmem = pl.BlockSpec(memory_space=pltpu.VMEM)
    return pl.pallas_call(
        send_back_kernel,
        in_specs=[pl.BlockSpec(memory_space=pltpu.SMEM)] + [vmem] * 6,
        out_specs=[vmem, vmem],
        out_shape=[
            jax.ShapeDtypeStruct((places, quarter, width), BF16),
            jax.ShapeDtypeStruct((quarter, width), BF16),
        ],
        scratch_shapes=[pltpu.VMEM((places, quarter, width), F32)],
        interpret=interpret,
        compiler_params=pltpu.CompilerParams(vmem_limit_bytes=40 * 2**20),
        name="send_back",
    )(at, *low, *high)


def by_owner_kernel(at_ref, in_ref, *refs):
    out_refs, total = refs[:-1], refs[-1]
    total[...] = jnp.zeros_like(total)
    for slot in range(in_ref.shape[0]):
        total[at_ref[slot]] += wide(in_ref[slot])
    blocks = out_refs[0].shape[0]
    for j, out_ref in enumerate(out_refs):
        out_ref[...] = narrow(total[j * blocks : (j + 1) * blocks])


def by_owner(at, received, blocks, interpret=False):
    _, quarter, width = received.shape
    vmem = pl.BlockSpec(memory_space=pltpu.VMEM)
    return pl.pallas_call(
        by_owner_kernel,
        in_specs=[pl.BlockSpec(memory_space=pltpu.SMEM), vmem],
        out_specs=[vmem] * Z,
        out_shape=[jax.ShapeDtypeStruct((blocks, quarter, width), BF16)] * Z,
        scratch_shapes=[pltpu.VMEM((Z * blocks + 1, quarter, width), F32)],
        interpret=interpret,
        compiler_params=pltpu.CompilerParams(vmem_limit_bytes=40 * 2**20),
        name="by_owner",
    )(at, received)


def fold_core_kernel(at_ref, terms_ref, arrived_ref, *out_refs):
    for j, out_ref in enumerate(out_refs):
        y = (at_ref[0] + j) % Y
        out_ref[...] = narrow(wide(terms_ref[y, at_ref[1]]) + wide(arrived_ref[y]))


def fold_core(y, c, terms, arrived):
    vmem = pl.BlockSpec(memory_space=pltpu.VMEM)
    return pl.pallas_call(
        fold_core_kernel,
        in_specs=[pl.BlockSpec(memory_space=pltpu.SMEM), vmem, vmem],
        out_specs=[vmem] * Y,
        out_shape=[jax.ShapeDtypeStruct(terms.shape[2:], BF16)] * Y,
        name="fold_core",
    )(jnp.stack([y, c]), terms, arrived)


def fold_y_kernel(z_ref, *refs):
    terms, out_refs = refs[:Y], refs[Y:]
    lines = out_refs[0].shape[0]
    for j, out_ref in enumerate(out_refs):
        part = pl.ds((z_ref[0] + j) % Z * lines, lines)
        total = wide(terms[0][part])
        for term in terms[1:]:
            total += wide(term[part])
        out_ref[...] = narrow(total)


def fold_y(z, terms):
    lines, v_dim = terms[0].shape
    vmem = pl.BlockSpec(memory_space=pltpu.VMEM)
    return pl.pallas_call(
        fold_y_kernel,
        in_specs=[pl.BlockSpec(memory_space=pltpu.SMEM)] + [vmem] * Y,
        out_specs=[vmem] * Z,
        out_shape=[jax.ShapeDtypeStruct((lines // Z, v_dim), BF16)] * Z,
        name="fold_y",
    )(z.reshape(1), *terms)


def copies_kernel(z_ref, *refs):
    pieces, out_ref = refs[:-1], refs[-1]
    lines = pieces[0].shape[0]
    for j, piece in enumerate(pieces):
        part = pl.ds((z_ref[0] + j) % Z * lines, lines)
        for peer in range(out_ref.shape[0]):
            out_ref[peer, part] = piece[...]


def copies(z, pieces):
    lines, v_dim = pieces[0].shape
    vmem = pl.BlockSpec(memory_space=pltpu.VMEM)
    return pl.pallas_call(
        copies_kernel,
        in_specs=[pl.BlockSpec(memory_space=pltpu.SMEM)] + [vmem] * Z,
        out_specs=vmem,
        out_shape=jax.ShapeDtypeStruct((Y * C, Z * lines, v_dim), BF16),
        name="copies",
    )(z.reshape(1), *pieces)


def local(query, cache, grad_out, value_weight, picked):
    q_dev, heads_here, width = query.shape
    block_count = cache.shape[0] // BLOCK
    seq = lax.axis_index("seq")
    x = lax.axis_index("head")
    z, y, c = seq // (Y * C), seq // C % Y, seq % C
    peers = Y * C
    quarter = BLOCK // X
    g_here = q_dev // QB
    others = g_here * OTHERS
    rows = q_dev * heads_here

    own_id = FIRST_OWN_OWNER * block_count + seq
    is_other = picked != own_id
    rank = jnp.cumsum(is_other.astype(jnp.int32), axis=1) - 1
    at_rank = is_other[:, :, None] & (rank[:, :, None] == jnp.arange(OTHERS, dtype=jnp.int32))
    ids = jnp.sum(jnp.where(at_rank, picked[:, :, None], 0), axis=1).reshape(others)
    owner, block = ids // block_count, ids % block_count
    place = owner % peers * Z_FULL + owner // peers
    places = peers * Z_FULL
    asked = place[:, None] == jnp.arange(places, dtype=jnp.int32)[None, :]
    wanted = jnp.max(jnp.where(asked, block[:, None], -1), axis=0)
    asked_here = trade_yc(wanted.reshape(peers, 1, Z_FULL)).reshape(peers, Z_FULL)
    z_off = (jnp.arange(Z_FULL, dtype=jnp.int32) - z) % Z
    valid = (asked_here >= 0).reshape(places)
    at_piece = (z_off[None, :] * block_count + asked_here).reshape(places)

    part_rows = jnp.arange(block_count * quarter, dtype=jnp.int32)
    part_rows = part_rows // quarter * BLOCK + x * quarter + part_rows % quarter
    take_part = part_rows[:, None] == jnp.arange(cache.shape[0], dtype=jnp.int32)[None, :]
    part = jnp.dot(take_part.astype(BF16), cache, preferred_element_type=F32)
    part = narrow(part).reshape(block_count, quarter, width)
    steps = (4, -3, 3, -2, 2, -1, 1)
    pieces = [part] + [None] * (Z - 1)
    for step in steps:
        pieces[-step % Z] = shift_z(part, step, lambda z: z < Z_FULL)
    owns = []
    for j in range(block_count):
        owns.append(
            lax.ppermute(
                part[j],
                "seq",
                [
                    (o, (o - FIRST_OWN_OWNER) * block_count + j)
                    for o in range(FIRST_OWN_OWNER, Z * peers)
                ],
            )
        )
    packed = pack(jnp.maximum(asked_here, 0).reshape(places), z, pieces)
    fetched = trade_yc(packed.reshape(peers, Z_FULL, quarter, width))
    d_latent = narrow(
        jnp.einsum("qhv,hcv->qhc", grad_out, value_weight, preferred_element_type=F32)
    )
    fetched, d_latent, query_rows = lax.optimization_barrier(
        (fetched, d_latent.reshape(rows, KVL), query.reshape(rows, width))
    )
    low, high = pick(place, seq % block_count, fetched.reshape(places, quarter, width), owns)

    low_from_left = shift_x(low, 1)
    high_from_right = shift_x(high, -1)
    low_from_right = shift_x(low, -1)
    high_from_left = shift_x(high, 1)
    low_far = shift_x(low_from_left, 1)
    high_far = shift_x(high_from_right, -1)

    d_query, latent_out, *d_keys = attend(
        x,
        query_rows,
        d_latent,
        [low, low_from_left, low_far, low_from_right],
        [high, high_from_left, high_far, high_from_right],
    )
    d_low, d_high = d_keys[:X], d_keys[X:]

    low_relay = shift_x(d_low[2], -1)
    high_relay = shift_x(d_high[2], 1)
    high_left = shift_x(d_high[1], -1)
    low_right = shift_x(d_low[3], 1)
    low_pair = narrow(wide(low_relay) + wide(d_low[1]))
    high_pair = narrow(wide(high_relay) + wide(d_high[3]))
    low_left = shift_x(low_pair, -1)
    high_right = shift_x(high_pair, 1)

    terms = narrow(
        jnp.einsum(
            "qhc,qhv->hcv",
            latent_out.reshape(q_dev, heads_here, KVL),
            grad_out,
            preferred_element_type=F32,
        )
    )
    v_dim = terms.shape[-1]
    terms = terms.reshape(Y, C, -1, v_dim)
    arrived = swap_core(lax.dynamic_index_in_dim(terms, 1 - c, 1, keepdims=False))
    folded = list(fold_core(y, c, terms, arrived))
    for step in (2, -1, 1):
        folded[step % Y] = shift_y(folded[step % Y], step)
    folded = fold_y(z, folded)
    total = wide(folded[0])
    for step in steps:
        total = total + wide(shift_z(folded[step % Z], step))
    total = narrow(total)
    pieces = [total] * Z
    for step in steps:
        pieces[-step % Z] = shift_z(total, step)
    terms = trade_yc(copies(z, pieces))
    d_value_weight = terms.reshape(value_weight.shape)

    back, own_share = send_back(
        place, [d_low[0], low_right, low_left], [d_high[0], high_left, high_right], places
    )
    received = trade_yc(back.reshape(peers, Z_FULL, quarter, width))
    own_back = []
    for j in range(block_count):
        own_back.append(
            lax.ppermute(
                own_share,
                "seq",
                [
                    ((o - FIRST_OWN_OWNER) * block_count + j, o)
                    for o in range(FIRST_OWN_OWNER, Z * peers)
                ],
            )
        )
    by_z = by_owner(
        jnp.where(valid, at_piece, Z * block_count),
        received.reshape(places, quarter, width),
        block_count,
    )
    d_cache = wide(by_z[0]) + wide(jnp.stack(own_back))
    for step in steps:
        arrived = shift_z(by_z[step % Z], step, lambda z: (z + step) % Z < Z_FULL)
        d_cache = d_cache + wide(arrived)
    return d_query.reshape(query.shape), d_cache, d_value_weight


def solution(mesh):
    in_specs = (
        P("seq", "head", None),
        P("seq", None),
        P("seq", "head", None),
        P("head", None, None),
        P("seq", None),
    )
    out_specs = (P("seq", "head", None), P("seq", "head", None), P("head", None, None))
    return jax.shard_map(local, mesh=mesh, in_specs=in_specs, out_specs=out_specs, check_vma=False)
```

```python
import jax
import jax.numpy as jnp
from jax import lax
from jax.experimental import pallas as pl
from jax.experimental.pallas import tpu as pltpu
from jax.sharding import PartitionSpec as P

KVL = 512
BLOCK = 128
QB = 32
TOPB = 4
OTHERS = TOPB - 1

SCORE_SCALE = 0.07216878364870323
MASKED = -1e30

Z, Y, C = 8, 4, 2
X = 4
Z_FULL = 6
FIRST_OWN_OWNER = Z_FULL * Y * C


F32 = jnp.float32
BF16 = jnp.bfloat16


def seq_of(z, y, c):
    return ((z % Z) * Y + y % Y) * C + c


def shift_z(array, step, sends=lambda z: True):
    pairs = [
        (seq_of(z, y, c), seq_of(z + step, y, c))
        for z in range(Z)
        for y in range(Y)
        for c in range(C)
        if sends(z)
    ]
    return lax.ppermute(array, "seq", pairs)


def gather_z(own, limit):
    right, left = [own], [own]
    for hop in range(4):
        right.append(shift_z(right[-1], 1, lambda z: (z - hop) % Z < limit))
        if hop < 3:
            left.append(shift_z(left[-1], -1, lambda z: (z + hop) % Z < limit))
    return [own, left[1], left[2], left[3], right[4], right[3], right[2], right[1]]


def reduce_z(terms, limit):
    right, left = terms[4], terms[5]
    for hop in range(4):
        right = shift_z(right, 1, lambda z: (z + 4 - hop) % Z < limit)
        if hop < 3:
            right = narrow(wide(right) + wide(terms[3 - hop]))
            left = shift_z(left, -1, lambda z: (z - 3 + hop) % Z < limit)
        if hop < 2:
            left = narrow(wide(left) + wide(terms[6 + hop]))
    return wide(terms[0]) + wide(right) + wide(left)


def shift_yc(array, y_step, c_step):
    pairs = [
        (seq_of(z, y, c), seq_of(z, y + y_step, c ^ c_step))
        for z in range(Z)
        for y in range(Y)
        for c in range(C)
    ]
    return lax.ppermute(array, "seq", pairs)


def swap_core(array):
    return lax.ppermute(array, "seq", [(s, s ^ 1) for s in range(Z * Y * C)])


def shift_x(array, step):
    return lax.ppermute(array, "head", [(x, (x + step) % X) for x in range(X)])


def trade(blocks, groups):
    return lax.all_to_all(
        blocks, "seq", split_axis=0, concat_axis=0, axis_index_groups=groups, tiled=True
    )


YC_GROUPS = [[seq_of(z, y, c) for y in range(Y) for c in range(C)] for z in range(Z)]
Y_GROUPS = [[seq_of(z, y, c) for y in range(Y)] for z in range(Z) for c in range(C)]
Z_GROUPS = [[seq_of(z, y, c) for z in range(Z)] for y in range(Y) for c in range(C)]


def narrow(array):
    return array.astype(BF16)


def wide(array):
    return array.astype(F32)


def pack_kernel(block_ref, z_ref, *refs):
    pieces, out_ref = refs[:Z], refs[Z]
    for j in range(Z):
        owner_z = (z_ref[0] + j) % Z

        @pl.when(owner_z < Z_FULL)
        def _():
            for peer in range(Y * C):
                place = peer * Z_FULL + owner_z
                out_ref[place] = pieces[j][block_ref[place]]


def pack(blocks, z, pieces):
    vmem = pl.BlockSpec(memory_space=pltpu.VMEM)
    smem = pl.BlockSpec(memory_space=pltpu.SMEM)
    return pl.pallas_call(
        pack_kernel,
        in_specs=[smem, smem] + [vmem] * Z,
        out_specs=vmem,
        out_shape=jax.ShapeDtypeStruct((blocks.shape[0], *pieces[0].shape[1:]), BF16),
        name="pack",
    )(blocks, z.reshape(1), *pieces)


def pick_kernel(place_ref, own_ref, fetched_ref, *refs):
    owns, (low_ref, high_ref) = refs[:-2], refs[-2:]
    n_low, n_high = low_ref.shape[0], high_ref.shape[0]
    for j, own in enumerate(owns):

        @pl.when(own_ref[0] == j)
        def _():
            low_ref[n_low - 1] = own[...]

    for slot in range(n_low - 1):
        low_ref[slot] = fetched_ref[place_ref[slot]]
    for slot in range(n_high):
        high_ref[slot] = fetched_ref[place_ref[n_low - 1 + slot]]


def pick(place, own_index, fetched, owns):
    vmem = pl.BlockSpec(memory_space=pltpu.VMEM)
    smem = pl.BlockSpec(memory_space=pltpu.SMEM)
    n_high = place.shape[0] // 2
    n_low = place.shape[0] - n_high + 1
    return pl.pallas_call(
        pick_kernel,
        in_specs=[smem, smem, vmem] + [vmem] * len(owns),
        out_specs=[vmem, vmem],
        out_shape=[
            jax.ShapeDtypeStruct((n_low, *fetched.shape[1:]), BF16),
            jax.ShapeDtypeStruct((n_high, *fetched.shape[1:]), BF16),
        ],
        name="pick",
    )(place, own_index.reshape(1), fetched, *owns)


def attend_kernel(x_ref, q_ref, dl_ref, *refs):
    low_refs, own_refs, high_refs = refs[:X], refs[X : 2 * X], refs[2 * X : 3 * X]
    dq_ref, lat_ref = refs[3 * X : 3 * X + 2]
    d_low_refs, d_high_refs = refs[3 * X + 2 : 4 * X + 2], refs[4 * X + 2 : 5 * X + 2]
    keys, own_sum = refs[5 * X + 2 :]
    block = pl.program_id(0)
    half_blocks = pl.num_programs(0) // 2
    rows, width = q_ref.shape
    heads = rows // QB
    quarter = own_refs[0].shape[1]
    n_part = OTHERS * quarter
    n_other = X * n_part

    @pl.when(block < half_blocks)
    def _():
        for j in range(X):
            keys[j * n_part : (j + 1) * n_part] = low_refs[j][...].reshape(n_part, width)

    @pl.when(block >= half_blocks)
    def _():
        for j in range(X):
            keys[j * n_part : (j + 1) * n_part] = high_refs[j][...].reshape(n_part, width)

    @pl.when(block == 0)
    def _():
        for j in range(X):
            keys[n_other + j * quarter : n_other + (j + 1) * quarter] = own_refs[j][0]

    q = q_ref[...]
    dl = dl_ref[...]
    k = keys[...]
    v = keys[:, :KVL]
    n_keys = k.shape[0]
    scores = lax.dot_general(q, k, (((1,), (1,)), ((), ())), preferred_element_type=F32)
    scores = scores * SCORE_SCALE
    col = lax.broadcasted_iota(jnp.int32, (rows, n_keys - n_other), 1)
    row = lax.broadcasted_iota(jnp.int32, (rows, n_keys - n_other), 0)
    source = (x_ref[0] + X - col // quarter) % X
    visible = source * quarter + col % quarter <= block * QB + row // heads
    scores = jnp.concatenate(
        [scores[:, :n_other], jnp.where(visible, scores[:, n_other:], MASKED)], axis=1
    )
    row_max = jnp.max(scores, axis=1, keepdims=True)
    exp_scores = jnp.exp(scores - row_max)
    weights = exp_scores / jnp.sum(exp_scores, axis=1, keepdims=True)
    weights_low = narrow(weights)
    latent = narrow(jnp.dot(weights_low, v, preferred_element_type=F32))
    lat_ref[...] = latent
    delta = jnp.sum(wide(dl) * wide(latent), axis=1, keepdims=True)
    d_probs = lax.dot_general(dl, v, (((1,), (1,)), ((), ())), preferred_element_type=F32)
    d_scores = narrow(SCORE_SCALE * weights * (d_probs - delta))
    dq_ref[...] = narrow(jnp.dot(d_scores, k, preferred_element_type=F32))
    d_keys = lax.dot_general(d_scores, q, (((0,), (0,)), ((), ())), preferred_element_type=F32)
    d_values = lax.dot_general(
        weights_low, dl, (((0,), (0,)), ((), ())), preferred_element_type=F32
    )
    d_keys = jnp.concatenate([d_keys[:, :KVL] + d_values, d_keys[:, KVL:]], axis=1)
    d_other = narrow(d_keys[:n_other]).reshape(X, OTHERS, quarter, width)

    @pl.when(block < half_blocks)
    def _():
        for j in range(X):
            d_low_refs[j][pl.ds(OTHERS * block, OTHERS)] = d_other[j]

    @pl.when(block >= half_blocks)
    def _():
        for j in range(X):
            d_high_refs[j][pl.ds(OTHERS * (block - half_blocks), OTHERS)] = d_other[j]

    d_own = d_keys[n_other:]

    @pl.when(block == 0)
    def _():
        own_sum[...] = d_own

    @pl.when(block > 0)
    def _():
        own_sum[...] += d_own

    @pl.when(block == pl.num_programs(0) - 1)
    def _():
        last = d_low_refs[0].shape[0] - 1
        for j in range(X):
            d_low_refs[j][last] = narrow(own_sum[j * quarter : (j + 1) * quarter])


def attend(x, q, dl, low, high, interpret=False):
    rows, width = q.shape
    n_low, quarter, _ = low[0].shape
    n_high = high[0].shape[0]
    blocks = (n_low - 1 + n_high) // OTHERS
    half = blocks // 2
    per = rows // blocks
    n_keys = TOPB * X * quarter
    part = (OTHERS, quarter, width)
    return pl.pallas_call(
        attend_kernel,
        grid_spec=pltpu.PrefetchScalarGridSpec(
            num_scalar_prefetch=1,
            grid=(blocks,),
            in_specs=[
                pl.BlockSpec((per, width), lambda g, x: (g, 0)),
                pl.BlockSpec((per, KVL), lambda g, x: (g, 0)),
            ]
            + [pl.BlockSpec(part, lambda g, x: (jnp.minimum(g, half - 1), 0, 0))] * X
            + [pl.BlockSpec((1, quarter, width), lambda g, x: (n_low - 1, 0, 0))] * X
            + [pl.BlockSpec(part, lambda g, x: (jnp.maximum(g - half, 0), 0, 0))] * X,
            out_specs=[
                pl.BlockSpec((per, width), lambda g, x: (g, 0)),
                pl.BlockSpec((per, KVL), lambda g, x: (g, 0)),
            ]
            + [pl.BlockSpec((n_low, quarter, width), lambda g, x: (0, 0, 0))] * X
            + [pl.BlockSpec((n_high, quarter, width), lambda g, x: (0, 0, 0))] * X,
            scratch_shapes=[
                pltpu.VMEM((n_keys, width), BF16),
                pltpu.VMEM((X * quarter, width), F32),
            ],
        ),
        out_shape=[
            jax.ShapeDtypeStruct((rows, width), BF16),
            jax.ShapeDtypeStruct((rows, KVL), BF16),
        ]
        + [jax.ShapeDtypeStruct((n_low, quarter, width), BF16)] * X
        + [jax.ShapeDtypeStruct((n_high, quarter, width), BF16)] * X,
        interpret=interpret,
        compiler_params=pltpu.CompilerParams(vmem_limit_bytes=56 * 2**20),
        name="attend",
    )(x.reshape(1), q, dl, *low, *low, *high)


def send_back_kernel(at_ref, *refs):
    low_refs, high_refs = refs[:3], refs[3:6]
    out_refs, own_ref, total = refs[6:-2], refs[-2], refs[-1]
    n_low, n_high = low_refs[0].shape[0], high_refs[0].shape[0]
    total[...] = jnp.zeros_like(total)
    for slot in range(n_low + n_high - 1):
        refs_here, index = (low_refs, slot) if slot < n_low - 1 else (high_refs, slot - n_low + 1)
        share = wide(refs_here[0][index]) + wide(refs_here[1][index]) + wide(refs_here[2][index])
        total[at_ref[slot]] += share
    last = n_low - 1
    own_ref[...] = narrow(
        wide(low_refs[0][last]) + wide(low_refs[1][last]) + wide(low_refs[2][last])
    )
    for j, out_ref in enumerate(out_refs):
        out_ref[...] = narrow(total[j * Z_FULL : (j + 1) * Z_FULL])


def send_back(at, low, high):
    _, quarter, width = low[0].shape
    vmem = pl.BlockSpec(memory_space=pltpu.VMEM)
    return pl.pallas_call(
        send_back_kernel,
        in_specs=[pl.BlockSpec(memory_space=pltpu.SMEM)] + [vmem] * 6,
        out_specs=[vmem] * (Y * C + 1),
        out_shape=[jax.ShapeDtypeStruct((Z_FULL, quarter, width), BF16)] * (Y * C)
        + [jax.ShapeDtypeStruct((quarter, width), BF16)],
        scratch_shapes=[pltpu.VMEM((Y * C * Z_FULL, quarter, width), F32)],
        compiler_params=pltpu.CompilerParams(vmem_limit_bytes=40 * 2**20),
        name="send_back",
    )(at, *low, *high)


def by_owner_kernel(at_ref, *refs):
    in_refs, out_refs, total = refs[: Y * C], refs[Y * C : -1], refs[-1]
    total[...] = jnp.zeros_like(total)
    for i, in_ref in enumerate(in_refs):
        for slot in range(Z_FULL):
            total[at_ref[i * Z_FULL + slot]] += wide(in_ref[slot])
    blocks = out_refs[0].shape[0]
    for j, out_ref in enumerate(out_refs):
        out_ref[...] = narrow(total[j * blocks : (j + 1) * blocks])


def by_owner(at, received, blocks):
    _, quarter, width = received[0].shape
    vmem = pl.BlockSpec(memory_space=pltpu.VMEM)
    return pl.pallas_call(
        by_owner_kernel,
        in_specs=[pl.BlockSpec(memory_space=pltpu.SMEM)] + [vmem] * (Y * C),
        out_specs=[vmem] * Z,
        out_shape=[jax.ShapeDtypeStruct((blocks, quarter, width), BF16)] * Z,
        scratch_shapes=[pltpu.VMEM((Z * blocks + 1, quarter, width), F32)],
        compiler_params=pltpu.CompilerParams(vmem_limit_bytes=40 * 2**20),
        name="by_owner",
    )(at, *received)


def local(query, cache, grad_out, value_weight, picked):
    q_dev, heads_here, width = query.shape
    block_count = cache.shape[0] // BLOCK
    seq = lax.axis_index("seq")
    x = lax.axis_index("head")
    z, y, c = seq // (Y * C), seq // C % Y, seq % C
    peers = Y * C
    quarter = BLOCK // X
    g_here = q_dev // QB
    others = g_here * OTHERS
    rows = q_dev * heads_here

    own_id = FIRST_OWN_OWNER * block_count + seq
    is_other = picked != own_id
    rank = jnp.cumsum(is_other.astype(jnp.int32), axis=1) - 1
    at_rank = is_other[:, :, None] & (rank[:, :, None] == jnp.arange(OTHERS, dtype=jnp.int32))
    ids = jnp.sum(jnp.where(at_rank, picked[:, :, None], 0), axis=1).reshape(others)
    owner, block = ids // block_count, ids % block_count
    place = owner % peers * Z_FULL + owner // peers
    places = peers * Z_FULL
    asked = place[:, None] == jnp.arange(places, dtype=jnp.int32)[None, :]
    wanted = jnp.max(jnp.where(asked, block[:, None], -1), axis=0)
    asked_here = trade(wanted.reshape(peers, 1, Z_FULL), YC_GROUPS).reshape(peers, Z_FULL)
    z_off = (jnp.arange(Z_FULL, dtype=jnp.int32) - z) % Z
    distance = jnp.arange(peers, dtype=jnp.int32)
    from_peer = (y - distance // C) % Y * C + (c ^ distance % C)
    pick_peer = from_peer[:, None, None] == jnp.arange(peers, dtype=jnp.int32)[None, :, None]
    asked_from = jnp.sum(jnp.where(pick_peer, asked_here[None], 0), axis=1)
    at_owner = jnp.where(
        asked_from >= 0, z_off[None, :] * block_count + asked_from, Z * block_count
    ).reshape(places)
    place_back = (owner // C % Y - y) % Y * C + (owner % C ^ c)
    place_back = place_back * Z_FULL + owner // peers

    part_rows = jnp.arange(block_count * quarter, dtype=jnp.int32)
    part_rows = part_rows // quarter * BLOCK + x * quarter + part_rows % quarter
    take_part = part_rows[:, None] == jnp.arange(cache.shape[0], dtype=jnp.int32)[None, :]
    part = jnp.dot(take_part.astype(BF16), cache, preferred_element_type=F32)
    part = narrow(part).reshape(block_count, quarter, width)
    pieces = gather_z(part, Z_FULL)
    owns = []
    for j in range(block_count):
        owns.append(
            lax.ppermute(
                part[j],
                "seq",
                [
                    (o, (o - FIRST_OWN_OWNER) * block_count + j)
                    for o in range(FIRST_OWN_OWNER, Z * peers)
                ],
            )
        )
    packed = pack(jnp.maximum(asked_here, 0).reshape(places), z, pieces)
    fetched = trade(packed.reshape(peers, Z_FULL, quarter, width), YC_GROUPS)
    d_latent = narrow(
        jnp.einsum("qhv,hcv->qhc", grad_out, value_weight, preferred_element_type=F32)
    )
    fetched, d_latent, query_rows = lax.optimization_barrier(
        (fetched, d_latent.reshape(rows, KVL), query.reshape(rows, width))
    )
    low, high = pick(place, seq % block_count, fetched.reshape(places, quarter, width), owns)

    low_from_left = shift_x(low, 1)
    high_from_right = shift_x(high, -1)
    low_from_right = shift_x(low, -1)
    high_from_left = shift_x(high, 1)
    low_far = shift_x(low_from_left, 1)
    high_far = shift_x(high_from_right, -1)

    d_query, latent_out, *d_keys = attend(
        x,
        query_rows,
        d_latent,
        [low, low_from_left, low_far, low_from_right],
        [high, high_from_left, high_far, high_from_right],
    )
    d_low, d_high = d_keys[:X], d_keys[X:]

    low_relay = shift_x(d_low[2], -1)
    high_relay = shift_x(d_high[2], 1)
    high_left = shift_x(d_high[1], -1)
    low_right = shift_x(d_low[3], 1)
    low_pair = narrow(wide(low_relay) + wide(d_low[1]))
    high_pair = narrow(wide(high_relay) + wide(d_high[3]))
    low_left = shift_x(low_pair, -1)
    high_right = shift_x(high_pair, 1)

    terms = narrow(
        jnp.einsum(
            "qhc,qhv->hcv",
            latent_out.reshape(q_dev, heads_here, KVL),
            grad_out,
            preferred_element_type=F32,
        )
    )
    v_dim = terms.shape[-1]
    terms = terms.reshape(Y, C, -1, v_dim)
    arrived = swap_core(lax.dynamic_index_in_dim(terms, 1 - c, 1, keepdims=False))
    terms = lax.dynamic_index_in_dim(terms, c, 1, keepdims=False)
    terms = narrow(wide(terms) + wide(arrived))
    terms = trade(terms, Y_GROUPS)
    terms = narrow(jnp.sum(wide(terms), axis=0))
    terms = trade(terms.reshape(Z, -1, v_dim), Z_GROUPS)
    terms = narrow(jnp.sum(wide(terms), axis=0))
    terms = trade(jnp.broadcast_to(terms, (Z, *terms.shape)), Z_GROUPS).reshape(-1, v_dim)
    terms = trade(jnp.broadcast_to(terms, (peers, *terms.shape)), YC_GROUPS)
    d_value_weight = terms.reshape(value_weight.shape)

    *back, own_share = send_back(
        place_back, [d_low[0], low_right, low_left], [d_high[0], high_left, high_right]
    )
    received = [back[0]] + [None] * (peers - 1)
    for i in (5, 4, 3, 7, 2, 6, 1):
        received[i] = shift_yc(back[i], i // C, i % C)
    own_back = []
    for j in range(block_count):
        own_back.append(
            lax.ppermute(
                own_share,
                "seq",
                [
                    ((o - FIRST_OWN_OWNER) * block_count + j, o)
                    for o in range(FIRST_OWN_OWNER, Z * peers)
                ],
            )
        )
    d_query = jnp.transpose(d_query.reshape(query.shape), (1, 2, 0))
    received, d_query = lax.optimization_barrier((received, d_query))
    by_z = by_owner(at_owner, received, block_count)
    d_cache = reduce_z(by_z, Z_FULL) + wide(jnp.stack(own_back))
    return jnp.transpose(d_query, (2, 0, 1)), d_cache, d_value_weight


def solution(mesh):
    in_specs = (
        P("seq", "head", None),
        P("seq", None),
        P("seq", "head", None),
        P("head", None, None),
        P("seq", None),
    )
    out_specs = (P("seq", "head", None), P("seq", "head", None), P("head", None, None))
    return jax.shard_map(local, mesh=mesh, in_specs=in_specs, out_specs=out_specs, check_vma=False)
```

```python
import jax
import jax.numpy as jnp
from jax import lax
from jax.experimental import pallas as pl
from jax.experimental.pallas import tpu as pltpu
from jax.sharding import PartitionSpec as P

KVL = 512
BLOCK = 128
QB = 32
TOPB = 4
OTHERS = TOPB - 1

SCORE_SCALE = 0.07216878364870323
MASKED = -1e30

Z, Y, C = 8, 4, 2
X = 4
Z_FULL = 6
FIRST_OWN_OWNER = Z_FULL * Y * C


F32 = jnp.float32
BF16 = jnp.bfloat16


def seq_of(z, y, c):
    return ((z % Z) * Y + y % Y) * C + c


def shift_z(array, step, sends=lambda z: True):
    pairs = [
        (seq_of(z, y, c), seq_of(z + step, y, c))
        for z in range(Z)
        for y in range(Y)
        for c in range(C)
        if sends(z)
    ]
    return lax.ppermute(array, "seq", pairs)


def gather_z(own, limit):
    right_2 = shift_z(own, 2, lambda z: z < limit)
    left_2 = shift_z(own, -2, lambda z: z < limit)
    right_1 = shift_z(own, 1, lambda z: z < limit)
    left_1 = shift_z(own, -1, lambda z: z < limit)
    right_4 = shift_z(right_2, 2, lambda z: (z - 2) % Z < limit)
    left_3 = shift_z(left_2, -1, lambda z: (z + 2) % Z < limit)
    right_3 = shift_z(right_2, 1, lambda z: (z - 2) % Z < limit)
    return [own, left_1, left_2, left_3, right_4, right_3, right_2, right_1]


def reduce_z(terms, limit, beside):
    right_4 = shift_z(terms[4], 2, lambda z: (z + 4) % Z < limit)
    right_3 = shift_z(terms[3], 1, lambda z: (z + 3) % Z < limit)
    left_3 = shift_z(terms[5], -1, lambda z: (z - 3) % Z < limit)
    right_1 = shift_z(terms[1], 1, lambda z: (z + 1) % Z < limit)
    left_1 = shift_z(terms[7], -1, lambda z: (z - 1) % Z < limit)
    right_4, right_3, left_3, beside = lax.optimization_barrier((right_4, right_3, left_3, beside))
    right_2 = narrow(wide(terms[2]) + wide(right_3) + wide(right_4))
    left_2 = narrow(wide(terms[6]) + wide(left_3))
    right_2 = shift_z(right_2, 2, lambda z: (z + 2) % Z < limit)
    left_2 = shift_z(left_2, -2, lambda z: (z - 2) % Z < limit)
    total = wide(terms[0])
    for arrived in (right_1, left_1, right_2, left_2):
        total = total + wide(arrived)
    return total, beside


def shift_yc(array, y_step, c_step):
    pairs = [
        (seq_of(z, y, c), seq_of(z, y + y_step, c ^ c_step))
        for z in range(Z)
        for y in range(Y)
        for c in range(C)
    ]
    return lax.ppermute(array, "seq", pairs)


def swap_core(array):
    return lax.ppermute(array, "seq", [(s, s ^ 1) for s in range(Z * Y * C)])


def exchange_yc(blocks):
    relayed = shift_yc(blocks[5], -1, 1)
    arrived = [blocks[0]] + [None] * (Y * C - 1)
    for i in (4, 7, 3, 6, 2, 1):
        arrived[i] = shift_yc(blocks[i], i // C, i % C)
    arrived[5] = shift_yc(relayed, -1, 0)
    return arrived


def shift_x(array, step):
    return lax.ppermute(array, "head", [(x, (x + step) % X) for x in range(X)])


def trade(blocks, groups):
    return lax.all_to_all(
        blocks, "seq", split_axis=0, concat_axis=0, axis_index_groups=groups, tiled=True
    )


YC_GROUPS = [[seq_of(z, y, c) for y in range(Y) for c in range(C)] for z in range(Z)]
Y_GROUPS = [[seq_of(z, y, c) for y in range(Y)] for z in range(Z) for c in range(C)]
Z_GROUPS = [[seq_of(z, y, c) for z in range(Z)] for y in range(Y) for c in range(C)]


def narrow(array):
    return array.astype(BF16)


def wide(array):
    return array.astype(F32)


def pack_kernel(block_ref, z_ref, *refs):
    pieces, out_refs = refs[:Z], refs[Z:]
    for j in range(Z):
        owner_z = (z_ref[0] + j) % Z

        @pl.when(owner_z < Z_FULL)
        def _():
            for i, out_ref in enumerate(out_refs):
                out_ref[owner_z] = pieces[j][block_ref[i * Z_FULL + owner_z]]


def pack(blocks, z, pieces):
    vmem = pl.BlockSpec(memory_space=pltpu.VMEM)
    smem = pl.BlockSpec(memory_space=pltpu.SMEM)
    return pl.pallas_call(
        pack_kernel,
        in_specs=[smem, smem] + [vmem] * Z,
        out_specs=[vmem] * (Y * C),
        out_shape=[jax.ShapeDtypeStruct((Z_FULL, *pieces[0].shape[1:]), BF16)] * (Y * C),
        name="pack",
    )(blocks, z.reshape(1), *pieces)


def pick_kernel(place_ref, own_ref, *refs):
    fetched, owns = refs[: Y * C], refs[Y * C : -3]
    low_ref, high_ref, blocks = refs[-3:]
    n_low, n_high = low_ref.shape[0], high_ref.shape[0]
    for i, part in enumerate(fetched):
        blocks[i * Z_FULL : (i + 1) * Z_FULL] = part[...]
    for j, own in enumerate(owns):

        @pl.when(own_ref[0] == j)
        def _():
            low_ref[n_low - 1] = own[...]

    for slot in range(n_low - 1):
        low_ref[slot] = blocks[place_ref[slot]]
    for slot in range(n_high):
        high_ref[slot] = blocks[place_ref[n_low - 1 + slot]]


def pick(place, own_index, fetched, owns):
    vmem = pl.BlockSpec(memory_space=pltpu.VMEM)
    smem = pl.BlockSpec(memory_space=pltpu.SMEM)
    n_high = place.shape[0] // 2
    n_low = place.shape[0] - n_high + 1
    block = fetched[0].shape[1:]
    return pl.pallas_call(
        pick_kernel,
        in_specs=[smem, smem] + [vmem] * (len(fetched) + len(owns)),
        out_specs=[vmem, vmem],
        out_shape=[
            jax.ShapeDtypeStruct((n_low, *block), BF16),
            jax.ShapeDtypeStruct((n_high, *block), BF16),
        ],
        scratch_shapes=[pltpu.VMEM((Y * C * Z_FULL, *block), BF16)],
        name="pick",
    )(place, own_index.reshape(1), *fetched, *owns)


def attend_kernel(x_ref, q_ref, dl_ref, *refs):
    low_refs, own_refs, high_refs = refs[:X], refs[X : 2 * X], refs[2 * X : 3 * X]
    dq_ref, lat_ref = refs[3 * X : 3 * X + 2]
    d_low_refs, d_high_refs = refs[3 * X + 2 : 4 * X + 2], refs[4 * X + 2 : 5 * X + 2]
    keys, own_sum = refs[5 * X + 2 :]
    block = pl.program_id(0)
    half_blocks = pl.num_programs(0) // 2
    rows, width = q_ref.shape
    heads = rows // QB
    quarter = own_refs[0].shape[1]
    n_part = OTHERS * quarter
    n_other = X * n_part

    @pl.when(block < half_blocks)
    def _():
        for j in range(X):
            keys[j * n_part : (j + 1) * n_part] = low_refs[j][...].reshape(n_part, width)

    @pl.when(block >= half_blocks)
    def _():
        for j in range(X):
            keys[j * n_part : (j + 1) * n_part] = high_refs[j][...].reshape(n_part, width)

    @pl.when(block == 0)
    def _():
        for j in range(X):
            keys[n_other + j * quarter : n_other + (j + 1) * quarter] = own_refs[j][0]

    q = q_ref[...]
    dl = dl_ref[...]
    k = keys[...]
    v = keys[:, :KVL]
    n_keys = k.shape[0]
    scores = lax.dot_general(q, k, (((1,), (1,)), ((), ())), preferred_element_type=F32)
    scores = scores * SCORE_SCALE
    col = lax.broadcasted_iota(jnp.int32, (rows, n_keys - n_other), 1)
    row = lax.broadcasted_iota(jnp.int32, (rows, n_keys - n_other), 0)
    source = (x_ref[0] + X - col // quarter) % X
    visible = source * quarter + col % quarter <= block * QB + row // heads
    scores = jnp.concatenate(
        [scores[:, :n_other], jnp.where(visible, scores[:, n_other:], MASKED)], axis=1
    )
    row_max = jnp.max(scores, axis=1, keepdims=True)
    exp_scores = jnp.exp(scores - row_max)
    weights = exp_scores / jnp.sum(exp_scores, axis=1, keepdims=True)
    weights_low = narrow(weights)
    latent = narrow(jnp.dot(weights_low, v, preferred_element_type=F32))
    lat_ref[...] = latent
    delta = jnp.sum(wide(dl) * wide(latent), axis=1, keepdims=True)
    d_probs = lax.dot_general(dl, v, (((1,), (1,)), ((), ())), preferred_element_type=F32)
    d_scores = narrow(SCORE_SCALE * weights * (d_probs - delta))
    dq_ref[...] = narrow(jnp.dot(d_scores, k, preferred_element_type=F32))
    d_keys = lax.dot_general(d_scores, q, (((0,), (0,)), ((), ())), preferred_element_type=F32)
    d_values = lax.dot_general(
        weights_low, dl, (((0,), (0,)), ((), ())), preferred_element_type=F32
    )
    d_keys = jnp.concatenate([d_keys[:, :KVL] + d_values, d_keys[:, KVL:]], axis=1)
    d_other = narrow(d_keys[:n_other]).reshape(X, OTHERS, quarter, width)

    @pl.when(block < half_blocks)
    def _():
        for j in range(X):
            d_low_refs[j][pl.ds(OTHERS * block, OTHERS)] = d_other[j]

    @pl.when(block >= half_blocks)
    def _():
        for j in range(X):
            d_high_refs[j][pl.ds(OTHERS * (block - half_blocks), OTHERS)] = d_other[j]

    d_own = d_keys[n_other:]

    @pl.when(block == 0)
    def _():
        own_sum[...] = d_own

    @pl.when(block > 0)
    def _():
        own_sum[...] += d_own

    @pl.when(block == pl.num_programs(0) - 1)
    def _():
        last = d_low_refs[0].shape[0] - 1
        for j in range(X):
            d_low_refs[j][last] = narrow(own_sum[j * quarter : (j + 1) * quarter])


def attend(x, q, dl, low, high, interpret=False):
    rows, width = q.shape
    n_low, quarter, _ = low[0].shape
    n_high = high[0].shape[0]
    blocks = (n_low - 1 + n_high) // OTHERS
    half = blocks // 2
    per = rows // blocks
    n_keys = TOPB * X * quarter
    part = (OTHERS, quarter, width)
    return pl.pallas_call(
        attend_kernel,
        grid_spec=pltpu.PrefetchScalarGridSpec(
            num_scalar_prefetch=1,
            grid=(blocks,),
            in_specs=[
                pl.BlockSpec((per, width), lambda g, x: (g, 0)),
                pl.BlockSpec((per, KVL), lambda g, x: (g, 0)),
            ]
            + [pl.BlockSpec(part, lambda g, x: (jnp.minimum(g, half - 1), 0, 0))] * X
            + [pl.BlockSpec((1, quarter, width), lambda g, x: (n_low - 1, 0, 0))] * X
            + [pl.BlockSpec(part, lambda g, x: (jnp.maximum(g - half, 0), 0, 0))] * X,
            out_specs=[
                pl.BlockSpec((per, width), lambda g, x: (g, 0)),
                pl.BlockSpec((per, KVL), lambda g, x: (g, 0)),
            ]
            + [pl.BlockSpec((n_low, quarter, width), lambda g, x: (0, 0, 0))] * X
            + [pl.BlockSpec((n_high, quarter, width), lambda g, x: (0, 0, 0))] * X,
            scratch_shapes=[
                pltpu.VMEM((n_keys, width), BF16),
                pltpu.VMEM((X * quarter, width), F32),
            ],
        ),
        out_shape=[
            jax.ShapeDtypeStruct((rows, width), BF16),
            jax.ShapeDtypeStruct((rows, KVL), BF16),
        ]
        + [jax.ShapeDtypeStruct((n_low, quarter, width), BF16)] * X
        + [jax.ShapeDtypeStruct((n_high, quarter, width), BF16)] * X,
        interpret=interpret,
        compiler_params=pltpu.CompilerParams(vmem_limit_bytes=56 * 2**20),
        name="attend",
    )(x.reshape(1), q, dl, *low, *low, *high)


def send_back_kernel(at_ref, *refs):
    low_refs, high_refs = refs[:3], refs[3:6]
    out_refs, own_ref, total = refs[6:-2], refs[-2], refs[-1]
    n_low, n_high = low_refs[0].shape[0], high_refs[0].shape[0]
    total[...] = jnp.zeros_like(total)
    for slot in range(n_low + n_high - 1):
        refs_here, index = (low_refs, slot) if slot < n_low - 1 else (high_refs, slot - n_low + 1)
        share = wide(refs_here[0][index]) + wide(refs_here[1][index]) + wide(refs_here[2][index])
        total[at_ref[slot]] += share
    last = n_low - 1
    own_ref[...] = narrow(
        wide(low_refs[0][last]) + wide(low_refs[1][last]) + wide(low_refs[2][last])
    )
    for j, out_ref in enumerate(out_refs):
        out_ref[...] = narrow(total[j * Z_FULL : (j + 1) * Z_FULL])


def send_back(at, low, high):
    _, quarter, width = low[0].shape
    vmem = pl.BlockSpec(memory_space=pltpu.VMEM)
    return pl.pallas_call(
        send_back_kernel,
        in_specs=[pl.BlockSpec(memory_space=pltpu.SMEM)] + [vmem] * 6,
        out_specs=[vmem] * (Y * C + 1),
        out_shape=[jax.ShapeDtypeStruct((Z_FULL, quarter, width), BF16)] * (Y * C)
        + [jax.ShapeDtypeStruct((quarter, width), BF16)],
        scratch_shapes=[pltpu.VMEM((Y * C * Z_FULL, quarter, width), F32)],
        compiler_params=pltpu.CompilerParams(vmem_limit_bytes=40 * 2**20),
        name="send_back",
    )(at, *low, *high)


def by_owner_kernel(at_ref, *refs):
    in_refs, out_refs, total = refs[: Y * C], refs[Y * C : -1], refs[-1]
    total[...] = jnp.zeros_like(total)
    for i, in_ref in enumerate(in_refs):
        for slot in range(Z_FULL):
            total[at_ref[i * Z_FULL + slot]] += wide(in_ref[slot])
    blocks = out_refs[0].shape[0]
    for j, out_ref in enumerate(out_refs):
        out_ref[...] = narrow(total[j * blocks : (j + 1) * blocks])


def by_owner(at, received, blocks):
    _, quarter, width = received[0].shape
    vmem = pl.BlockSpec(memory_space=pltpu.VMEM)
    return pl.pallas_call(
        by_owner_kernel,
        in_specs=[pl.BlockSpec(memory_space=pltpu.SMEM)] + [vmem] * (Y * C),
        out_specs=[vmem] * Z,
        out_shape=[jax.ShapeDtypeStruct((blocks, quarter, width), BF16)] * Z,
        scratch_shapes=[pltpu.VMEM((Z * blocks + 1, quarter, width), F32)],
        compiler_params=pltpu.CompilerParams(vmem_limit_bytes=40 * 2**20),
        name="by_owner",
    )(at, *received)


def local(query, cache, grad_out, value_weight, picked):
    q_dev, heads_here, width = query.shape
    block_count = cache.shape[0] // BLOCK
    seq = lax.axis_index("seq")
    x = lax.axis_index("head")
    z, y, c = seq // (Y * C), seq // C % Y, seq % C
    peers = Y * C
    quarter = BLOCK // X
    g_here = q_dev // QB
    others = g_here * OTHERS
    rows = q_dev * heads_here

    own_id = FIRST_OWN_OWNER * block_count + seq
    is_other = picked != own_id
    rank = jnp.cumsum(is_other.astype(jnp.int32), axis=1) - 1
    at_rank = is_other[:, :, None] & (rank[:, :, None] == jnp.arange(OTHERS, dtype=jnp.int32))
    ids = jnp.sum(jnp.where(at_rank, picked[:, :, None], 0), axis=1).reshape(others)
    owner, block = ids // block_count, ids % block_count
    place = owner % peers * Z_FULL + owner // peers
    places = peers * Z_FULL
    asked = place[:, None] == jnp.arange(places, dtype=jnp.int32)[None, :]
    wanted = jnp.max(jnp.where(asked, block[:, None], -1), axis=0)
    asked_here = trade(wanted.reshape(peers, 1, Z_FULL), YC_GROUPS).reshape(peers, Z_FULL)
    z_off = (jnp.arange(Z_FULL, dtype=jnp.int32) - z) % Z
    distance = jnp.arange(peers, dtype=jnp.int32)
    peer_ids = jnp.arange(peers, dtype=jnp.int32)[None, :, None]
    to_peer = (y + distance // C) % Y * C + (c ^ distance % C)
    asked_to = jnp.sum(jnp.where(to_peer[:, None, None] == peer_ids, asked_here[None], 0), axis=1)
    from_peer = (y - distance // C) % Y * C + (c ^ distance % C)
    asked_from = jnp.sum(jnp.where(from_peer[:, None, None] == peer_ids, asked_here[None], 0), axis=1)
    at_owner = jnp.where(
        asked_from >= 0, z_off[None, :] * block_count + asked_from, Z * block_count
    ).reshape(places)
    place_fetched = (y - owner // C) % Y * C + (owner % C ^ c)
    place_fetched = place_fetched * Z_FULL + owner // peers
    place_back = (owner // C % Y - y) % Y * C + (owner % C ^ c)
    place_back = place_back * Z_FULL + owner // peers

    part_rows = jnp.arange(block_count * quarter, dtype=jnp.int32)
    part_rows = part_rows // quarter * BLOCK + x * quarter + part_rows % quarter
    take_part = part_rows[:, None] == jnp.arange(cache.shape[0], dtype=jnp.int32)[None, :]
    part = jnp.dot(take_part.astype(BF16), cache, preferred_element_type=F32)
    part = narrow(part).reshape(block_count, quarter, width)
    pieces = gather_z(part, Z_FULL)
    owns = []
    for j in range(block_count):
        owns.append(
            lax.ppermute(
                part[j],
                "seq",
                [
                    (o, (o - FIRST_OWN_OWNER) * block_count + j)
                    for o in range(FIRST_OWN_OWNER, Z * peers)
                ],
            )
        )
    packed = pack(jnp.maximum(asked_to, 0).reshape(places), z, pieces)
    packed, query = lax.optimization_barrier((packed, query))
    fetched = exchange_yc(packed)
    d_latent = narrow(
        jnp.einsum("qhv,hcv->qhc", grad_out, value_weight, preferred_element_type=F32)
    )
    fetched, d_latent, query_rows = lax.optimization_barrier(
        (fetched, d_latent.reshape(rows, KVL), query.reshape(rows, width))
    )
    low, high = pick(place_fetched, seq % block_count, fetched, owns)

    low_from_left = shift_x(low, 1)
    high_from_right = shift_x(high, -1)
    low_from_right = shift_x(low, -1)
    high_from_left = shift_x(high, 1)
    low_far = shift_x(low_from_left, 1)
    high_far = shift_x(high_from_right, -1)

    d_query, latent_out, *d_keys = attend(
        x,
        query_rows,
        d_latent,
        [low, low_from_left, low_far, low_from_right],
        [high, high_from_left, high_far, high_from_right],
    )
    d_low, d_high = d_keys[:X], d_keys[X:]

    low_relay = shift_x(d_low[2], -1)
    high_relay = shift_x(d_high[2], 1)
    high_left = shift_x(d_high[1], -1)
    low_right = shift_x(d_low[3], 1)
    low_pair = narrow(wide(low_relay) + wide(d_low[1]))
    high_pair = narrow(wide(high_relay) + wide(d_high[3]))
    low_left = shift_x(low_pair, -1)
    high_right = shift_x(high_pair, 1)

    terms = narrow(
        jnp.einsum(
            "qhc,qhv->hcv",
            latent_out.reshape(q_dev, heads_here, KVL),
            grad_out,
            preferred_element_type=F32,
        )
    )
    v_dim = terms.shape[-1]
    terms = terms.reshape(Y, C, -1, v_dim)
    arrived = swap_core(lax.dynamic_index_in_dim(terms, 1 - c, 1, keepdims=False))
    terms = lax.dynamic_index_in_dim(terms, c, 1, keepdims=False)
    terms = narrow(wide(terms) + wide(arrived))
    terms = trade(terms, Y_GROUPS)
    terms = narrow(jnp.sum(wide(terms), axis=0))
    terms = trade(terms.reshape(Z, -1, v_dim), Z_GROUPS)
    terms = narrow(jnp.sum(wide(terms), axis=0))
    terms = trade(jnp.broadcast_to(terms, (Z, *terms.shape)), Z_GROUPS).reshape(-1, v_dim)
    terms = trade(jnp.broadcast_to(terms, (peers, *terms.shape)), YC_GROUPS)
    d_value_weight = terms.reshape(value_weight.shape)

    *back, own_share = send_back(
        place_back, [d_low[0], low_right, low_left], [d_high[0], high_left, high_right]
    )
    received = exchange_yc(back)
    own_back = []
    for j in range(block_count):
        own_back.append(
            lax.ppermute(
                own_share,
                "seq",
                [
                    ((o - FIRST_OWN_OWNER) * block_count + j, o)
                    for o in range(FIRST_OWN_OWNER, Z * peers)
                ],
            )
        )
    d_query = jnp.transpose(d_query.reshape(query.shape), (1, 2, 0))
    by_z = by_owner(at_owner, received, block_count)
    d_cache, d_query = reduce_z(by_z, Z_FULL, d_query)
    d_cache = d_cache + wide(jnp.stack(own_back))
    return jnp.transpose(d_query, (2, 0, 1)), d_cache, d_value_weight


def solution(mesh):
    in_specs = (
        P("seq", "head", None),
        P("seq", None),
        P("seq", "head", None),
        P("head", None, None),
        P("seq", None),
    )
    out_specs = (P("seq", "head", None), P("seq", "head", None), P("head", None, None))
    return jax.shard_map(local, mesh=mesh, in_specs=in_specs, out_specs=out_specs, check_vma=False)
```

```python
import jax
import jax.numpy as jnp
from jax import lax
from jax.experimental import pallas as pl
from jax.experimental.pallas import tpu as pltpu
from jax.sharding import PartitionSpec as P

KVL = 512
BLOCK = 128
QB = 32
TOPB = 4
OTHERS = TOPB - 1

SCORE_SCALE = 0.07216878364870323
MASKED = -1e30

Z, Y, C = 8, 4, 2
X = 4
Z_FULL = 6
FIRST_OWN_OWNER = Z_FULL * Y * C


F32 = jnp.float32
BF16 = jnp.bfloat16


def seq_of(z, y, c):
    return ((z % Z) * Y + y % Y) * C + c


def shift_z(array, step, sends=lambda z: True):
    pairs = [
        (seq_of(z, y, c), seq_of(z + step, y, c))
        for z in range(Z)
        for y in range(Y)
        for c in range(C)
        if sends(z)
    ]
    return lax.ppermute(array, "seq", pairs)


def gather_z(own, limit):
    right, left = [own], [own]
    for hop in range(4):
        right.append(shift_z(right[-1], 1, lambda z: (z - hop) % Z < limit))
        if hop < 3:
            left.append(shift_z(left[-1], -1, lambda z: (z + hop) % Z < limit))
    return [own, left[1], left[2], left[3], right[4], right[3], right[2], right[1]]


def reduce_z(terms, limit, beside):
    right, left = terms[4], terms[5]
    for hop in range(4):
        right = shift_z(right, 1, lambda z: (z + 4 - hop) % Z < limit)
        if hop < 3:
            left = shift_z(left, -1, lambda z: (z - 3 + hop) % Z < limit)
        if hop == 0:
            right, left, beside = lax.optimization_barrier((right, left, beside))
        if hop < 3:
            right = narrow(wide(right) + wide(terms[3 - hop]))
        if hop < 2:
            left = narrow(wide(left) + wide(terms[6 + hop]))
    return wide(terms[0]) + wide(right) + wide(left), beside


def shift_yc(array, y_step, c_step):
    pairs = [
        (seq_of(z, y, c), seq_of(z, y + y_step, c ^ c_step))
        for z in range(Z)
        for y in range(Y)
        for c in range(C)
    ]
    return lax.ppermute(array, "seq", pairs)


def shift_x(array, step):
    return lax.ppermute(array, "head", [(x, (x + step) % X) for x in range(X)])


def trade(blocks, groups):
    return lax.all_to_all(
        blocks, "seq", split_axis=0, concat_axis=0, axis_index_groups=groups, tiled=True
    )


YC_GROUPS = [[seq_of(z, y, c) for y in range(Y) for c in range(C)] for z in range(Z)]
Z_GROUPS = [[seq_of(z, y, c) for z in range(Z)] for y in range(Y) for c in range(C)]


def narrow(array):
    return array.astype(BF16)


def wide(array):
    return array.astype(F32)


def pack_kernel(block_ref, z_ref, *refs):
    pieces, out_ref = refs[:Z], refs[Z]
    for j in range(Z):
        owner_z = (z_ref[0] + j) % Z

        @pl.when(owner_z < Z_FULL)
        def _():
            for peer in range(Y * C):
                place = peer * Z_FULL + owner_z
                out_ref[place] = pieces[j][block_ref[place]]


def pack(blocks, z, pieces):
    vmem = pl.BlockSpec(memory_space=pltpu.VMEM)
    smem = pl.BlockSpec(memory_space=pltpu.SMEM)
    return pl.pallas_call(
        pack_kernel,
        in_specs=[smem, smem] + [vmem] * Z,
        out_specs=vmem,
        out_shape=jax.ShapeDtypeStruct((blocks.shape[0], *pieces[0].shape[1:]), BF16),
        name="pack",
    )(blocks, z.reshape(1), *pieces)


def pick_kernel(place_ref, own_ref, fetched_ref, *refs):
    owns, (low_ref, high_ref) = refs[:-2], refs[-2:]
    n_low, n_high = low_ref.shape[0], high_ref.shape[0]
    for j, own in enumerate(owns):

        @pl.when(own_ref[0] == j)
        def _():
            low_ref[n_low - 1] = own[...]

    for slot in range(n_low - 1):
        low_ref[slot] = fetched_ref[place_ref[slot]]
    for slot in range(n_high):
        high_ref[slot] = fetched_ref[place_ref[n_low - 1 + slot]]


def pick(place, own_index, fetched, owns):
    vmem = pl.BlockSpec(memory_space=pltpu.VMEM)
    smem = pl.BlockSpec(memory_space=pltpu.SMEM)
    n_high = place.shape[0] // 2
    n_low = place.shape[0] - n_high + 1
    return pl.pallas_call(
        pick_kernel,
        in_specs=[smem, smem, vmem] + [vmem] * len(owns),
        out_specs=[vmem, vmem],
        out_shape=[
            jax.ShapeDtypeStruct((n_low, *fetched.shape[1:]), BF16),
            jax.ShapeDtypeStruct((n_high, *fetched.shape[1:]), BF16),
        ],
        name="pick",
    )(place, own_index.reshape(1), fetched, *owns)


def attend_kernel(x_ref, q_ref, dl_ref, *refs):
    low_refs, own_refs, high_refs = refs[:X], refs[X : 2 * X], refs[2 * X : 3 * X]
    dq_ref, lat_ref = refs[3 * X : 3 * X + 2]
    d_low_refs, d_high_refs = refs[3 * X + 2 : 4 * X + 2], refs[4 * X + 2 : 5 * X + 2]
    keys, own_sum = refs[5 * X + 2 :]
    block = pl.program_id(0)
    half_blocks = pl.num_programs(0) // 2
    rows, width = q_ref.shape
    heads = rows // QB
    quarter = own_refs[0].shape[1]
    n_part = OTHERS * quarter
    n_other = X * n_part

    @pl.when(block < half_blocks)
    def _():
        for j in range(X):
            keys[j * n_part : (j + 1) * n_part] = low_refs[j][...].reshape(n_part, width)

    @pl.when(block >= half_blocks)
    def _():
        for j in range(X):
            keys[j * n_part : (j + 1) * n_part] = high_refs[j][...].reshape(n_part, width)

    @pl.when(block == 0)
    def _():
        for j in range(X):
            keys[n_other + j * quarter : n_other + (j + 1) * quarter] = own_refs[j][0]

    q = q_ref[...]
    dl = dl_ref[...]
    k = keys[...]
    v = keys[:, :KVL]
    n_keys = k.shape[0]
    scores = lax.dot_general(q, k, (((1,), (1,)), ((), ())), preferred_element_type=F32)
    scores = scores * SCORE_SCALE
    col = lax.broadcasted_iota(jnp.int32, (rows, n_keys - n_other), 1)
    row = lax.broadcasted_iota(jnp.int32, (rows, n_keys - n_other), 0)
    source = (x_ref[0] + X - col // quarter) % X
    visible = source * quarter + col % quarter <= block * QB + row // heads
    scores = jnp.concatenate(
        [scores[:, :n_other], jnp.where(visible, scores[:, n_other:], MASKED)], axis=1
    )
    row_max = jnp.max(scores, axis=1, keepdims=True)
    exp_scores = jnp.exp(scores - row_max)
    weights = exp_scores / jnp.sum(exp_scores, axis=1, keepdims=True)
    weights_low = narrow(weights)
    latent = narrow(jnp.dot(weights_low, v, preferred_element_type=F32))
    lat_ref[...] = latent
    delta = jnp.sum(wide(dl) * wide(latent), axis=1, keepdims=True)
    d_probs = lax.dot_general(dl, v, (((1,), (1,)), ((), ())), preferred_element_type=F32)
    d_scores = narrow(SCORE_SCALE * weights * (d_probs - delta))
    dq_ref[...] = narrow(jnp.dot(d_scores, k, preferred_element_type=F32))
    d_keys = lax.dot_general(d_scores, q, (((0,), (0,)), ((), ())), preferred_element_type=F32)
    d_values = lax.dot_general(
        weights_low, dl, (((0,), (0,)), ((), ())), preferred_element_type=F32
    )
    d_keys = jnp.concatenate([d_keys[:, :KVL] + d_values, d_keys[:, KVL:]], axis=1)
    d_other = narrow(d_keys[:n_other]).reshape(X, OTHERS, quarter, width)

    @pl.when(block < half_blocks)
    def _():
        for j in range(X):
            d_low_refs[j][pl.ds(OTHERS * block, OTHERS)] = d_other[j]

    @pl.when(block >= half_blocks)
    def _():
        for j in range(X):
            d_high_refs[j][pl.ds(OTHERS * (block - half_blocks), OTHERS)] = d_other[j]

    d_own = d_keys[n_other:]

    @pl.when(block == 0)
    def _():
        own_sum[...] = d_own

    @pl.when(block > 0)
    def _():
        own_sum[...] += d_own

    @pl.when(block == pl.num_programs(0) - 1)
    def _():
        last = d_low_refs[0].shape[0] - 1
        for j in range(X):
            d_low_refs[j][last] = narrow(own_sum[j * quarter : (j + 1) * quarter])


def attend(x, q, dl, low, high, interpret=False):
    rows, width = q.shape
    n_low, quarter, _ = low[0].shape
    n_high = high[0].shape[0]
    blocks = (n_low - 1 + n_high) // OTHERS
    half = blocks // 2
    per = rows // blocks
    n_keys = TOPB * X * quarter
    part = (OTHERS, quarter, width)
    return pl.pallas_call(
        attend_kernel,
        grid_spec=pltpu.PrefetchScalarGridSpec(
            num_scalar_prefetch=1,
            grid=(blocks,),
            in_specs=[
                pl.BlockSpec((per, width), lambda g, x: (g, 0)),
                pl.BlockSpec((per, KVL), lambda g, x: (g, 0)),
            ]
            + [pl.BlockSpec(part, lambda g, x: (jnp.minimum(g, half - 1), 0, 0))] * X
            + [pl.BlockSpec((1, quarter, width), lambda g, x: (n_low - 1, 0, 0))] * X
            + [pl.BlockSpec(part, lambda g, x: (jnp.maximum(g - half, 0), 0, 0))] * X,
            out_specs=[
                pl.BlockSpec((per, width), lambda g, x: (g, 0)),
                pl.BlockSpec((per, KVL), lambda g, x: (g, 0)),
            ]
            + [pl.BlockSpec((n_low, quarter, width), lambda g, x: (0, 0, 0))] * X
            + [pl.BlockSpec((n_high, quarter, width), lambda g, x: (0, 0, 0))] * X,
            scratch_shapes=[
                pltpu.VMEM((n_keys, width), BF16),
                pltpu.VMEM((X * quarter, width), F32),
            ],
        ),
        out_shape=[
            jax.ShapeDtypeStruct((rows, width), BF16),
            jax.ShapeDtypeStruct((rows, KVL), BF16),
        ]
        + [jax.ShapeDtypeStruct((n_low, quarter, width), BF16)] * X
        + [jax.ShapeDtypeStruct((n_high, quarter, width), BF16)] * X,
        interpret=interpret,
        compiler_params=pltpu.CompilerParams(vmem_limit_bytes=56 * 2**20),
        name="attend",
    )(x.reshape(1), q, dl, *low, *low, *high)


def send_back_kernel(at_ref, *refs):
    low_refs, high_refs = refs[:3], refs[3:6]
    out_refs, own_ref, total = refs[6:-2], refs[-2], refs[-1]
    n_low, n_high = low_refs[0].shape[0], high_refs[0].shape[0]
    total[...] = jnp.zeros_like(total)
    for slot in range(n_low + n_high - 1):
        refs_here, index = (low_refs, slot) if slot < n_low - 1 else (high_refs, slot - n_low + 1)
        share = wide(refs_here[0][index]) + wide(refs_here[1][index]) + wide(refs_here[2][index])
        total[at_ref[slot]] += share
    last = n_low - 1
    own_ref[...] = narrow(
        wide(low_refs[0][last]) + wide(low_refs[1][last]) + wide(low_refs[2][last])
    )
    for j, out_ref in enumerate(out_refs):
        out_ref[...] = narrow(total[j * Z_FULL : (j + 1) * Z_FULL])


def send_back(at, low, high):
    _, quarter, width = low[0].shape
    vmem = pl.BlockSpec(memory_space=pltpu.VMEM)
    return pl.pallas_call(
        send_back_kernel,
        in_specs=[pl.BlockSpec(memory_space=pltpu.SMEM)] + [vmem] * 6,
        out_specs=[vmem] * (Y * C + 1),
        out_shape=[jax.ShapeDtypeStruct((Z_FULL, quarter, width), BF16)] * (Y * C)
        + [jax.ShapeDtypeStruct((quarter, width), BF16)],
        scratch_shapes=[pltpu.VMEM((Y * C * Z_FULL, quarter, width), F32)],
        compiler_params=pltpu.CompilerParams(vmem_limit_bytes=40 * 2**20),
        name="send_back",
    )(at, *low, *high)


def by_owner_kernel(at_ref, *refs):
    in_refs, out_refs, total = refs[: Y * C], refs[Y * C : -1], refs[-1]
    total[...] = jnp.zeros_like(total)
    for i, in_ref in enumerate(in_refs):
        for slot in range(Z_FULL):
            total[at_ref[i * Z_FULL + slot]] += wide(in_ref[slot])
    blocks = out_refs[0].shape[0]
    for j, out_ref in enumerate(out_refs):
        out_ref[...] = narrow(total[j * blocks : (j + 1) * blocks])


def by_owner(at, received, blocks):
    _, quarter, width = received[0].shape
    vmem = pl.BlockSpec(memory_space=pltpu.VMEM)
    return pl.pallas_call(
        by_owner_kernel,
        in_specs=[pl.BlockSpec(memory_space=pltpu.SMEM)] + [vmem] * (Y * C),
        out_specs=[vmem] * Z,
        out_shape=[jax.ShapeDtypeStruct((blocks, quarter, width), BF16)] * Z,
        scratch_shapes=[pltpu.VMEM((Z * blocks + 1, quarter, width), F32)],
        compiler_params=pltpu.CompilerParams(vmem_limit_bytes=40 * 2**20),
        name="by_owner",
    )(at, *received)


def local(query, cache, grad_out, value_weight, picked):
    q_dev, heads_here, width = query.shape
    block_count = cache.shape[0] // BLOCK
    seq = lax.axis_index("seq")
    x = lax.axis_index("head")
    z, y, c = seq // (Y * C), seq // C % Y, seq % C
    peers = Y * C
    quarter = BLOCK // X
    g_here = q_dev // QB
    others = g_here * OTHERS
    rows = q_dev * heads_here

    own_id = FIRST_OWN_OWNER * block_count + seq
    is_other = picked != own_id
    rank = jnp.cumsum(is_other.astype(jnp.int32), axis=1) - 1
    at_rank = is_other[:, :, None] & (rank[:, :, None] == jnp.arange(OTHERS, dtype=jnp.int32))
    ids = jnp.sum(jnp.where(at_rank, picked[:, :, None], 0), axis=1).reshape(others)
    owner, block = ids // block_count, ids % block_count
    place = owner % peers * Z_FULL + owner // peers
    places = peers * Z_FULL
    asked = place[:, None] == jnp.arange(places, dtype=jnp.int32)[None, :]
    wanted = jnp.max(jnp.where(asked, block[:, None], -1), axis=0)
    asked_here = trade(wanted.reshape(peers, 1, Z_FULL), YC_GROUPS).reshape(peers, Z_FULL)
    z_off = (jnp.arange(Z_FULL, dtype=jnp.int32) - z) % Z
    distance = jnp.arange(peers, dtype=jnp.int32)
    from_peer = (y - distance // C) % Y * C + (c ^ distance % C)
    pick_peer = from_peer[:, None, None] == jnp.arange(peers, dtype=jnp.int32)[None, :, None]
    asked_from = jnp.sum(jnp.where(pick_peer, asked_here[None], 0), axis=1)
    at_owner = jnp.where(
        asked_from >= 0, z_off[None, :] * block_count + asked_from, Z * block_count
    ).reshape(places)
    place_back = (owner // C % Y - y) % Y * C + (owner % C ^ c)
    place_back = place_back * Z_FULL + owner // peers

    part_rows = jnp.arange(block_count * quarter, dtype=jnp.int32)
    part_rows = part_rows // quarter * BLOCK + x * quarter + part_rows % quarter
    take_part = part_rows[:, None] == jnp.arange(cache.shape[0], dtype=jnp.int32)[None, :]
    part = jnp.dot(take_part.astype(BF16), cache, preferred_element_type=F32)
    part = narrow(part).reshape(block_count, quarter, width)
    pieces = gather_z(part, Z_FULL)
    owns = []
    for j in range(block_count):
        owns.append(
            lax.ppermute(
                part[j],
                "seq",
                [
                    (o, (o - FIRST_OWN_OWNER) * block_count + j)
                    for o in range(FIRST_OWN_OWNER, Z * peers)
                ],
            )
        )
    packed = pack(jnp.maximum(asked_here, 0).reshape(places), z, pieces)
    fetched = trade(packed.reshape(peers, Z_FULL, quarter, width), YC_GROUPS)
    d_latent = narrow(
        jnp.einsum("qhv,hcv->qhc", grad_out, value_weight, preferred_element_type=F32)
    )
    fetched, d_latent, query_rows = lax.optimization_barrier(
        (fetched, d_latent.reshape(rows, KVL), query.reshape(rows, width))
    )
    low, high = pick(place, seq % block_count, fetched.reshape(places, quarter, width), owns)

    low_from_left = shift_x(low, 1)
    high_from_right = shift_x(high, -1)
    low_from_right = shift_x(low, -1)
    high_from_left = shift_x(high, 1)
    low_far = shift_x(low_from_left, 1)
    high_far = shift_x(high_from_right, -1)

    d_query, latent_out, *d_keys = attend(
        x,
        query_rows,
        d_latent,
        [low, low_from_left, low_far, low_from_right],
        [high, high_from_left, high_far, high_from_right],
    )
    d_low, d_high = d_keys[:X], d_keys[X:]

    low_relay = shift_x(d_low[2], -1)
    high_relay = shift_x(d_high[2], 1)
    high_left = shift_x(d_high[1], -1)
    low_right = shift_x(d_low[3], 1)
    low_pair = narrow(wide(low_relay) + wide(d_low[1]))
    high_pair = narrow(wide(high_relay) + wide(d_high[3]))
    low_left = shift_x(low_pair, -1)
    high_right = shift_x(high_pair, 1)

    terms = narrow(
        jnp.einsum(
            "qhc,qhv->hcv",
            latent_out.reshape(q_dev, heads_here, KVL),
            grad_out,
            preferred_element_type=F32,
        )
    )
    v_dim = terms.shape[-1]
    terms = lax.all_to_all(
        terms.reshape(Z * peers, -1, v_dim), "seq", split_axis=0, concat_axis=0, tiled=True
    )
    terms = narrow(jnp.sum(wide(terms), axis=0))
    terms = trade(jnp.broadcast_to(terms, (Z, *terms.shape)), Z_GROUPS)
    terms = trade(jnp.broadcast_to(terms, (peers, *terms.shape)), YC_GROUPS)
    terms = jnp.swapaxes(terms, 0, 1)
    d_value_weight = terms.reshape(value_weight.shape)

    *back, own_share = send_back(
        place_back, [d_low[0], low_right, low_left], [d_high[0], high_left, high_right]
    )
    received = [back[0]] + [None] * (peers - 1)
    for i in (5, 4, 3, 7, 2, 6, 1):
        received[i] = shift_yc(back[i], i // C, i % C)
    own_back = []
    for j in range(block_count):
        own_back.append(
            lax.ppermute(
                own_share,
                "seq",
                [
                    ((o - FIRST_OWN_OWNER) * block_count + j, o)
                    for o in range(FIRST_OWN_OWNER, Z * peers)
                ],
            )
        )
    d_query = jnp.transpose(d_query.reshape(query.shape), (1, 2, 0))
    by_z = by_owner(at_owner, received, block_count)
    d_cache, d_query = reduce_z(by_z, Z_FULL, d_query)
    d_cache = d_cache + wide(jnp.stack(own_back))
    return jnp.transpose(d_query, (2, 0, 1)), d_cache, d_value_weight


def solution(mesh):
    in_specs = (
        P("seq", "head", None),
        P("seq", None),
        P("seq", "head", None),
        P("head", None, None),
        P("seq", None),
    )
    out_specs = (P("seq", "head", None), P("seq", "head", None), P("head", None, None))
    return jax.shard_map(local, mesh=mesh, in_specs=in_specs, out_specs=out_specs, check_vma=False)
```

```python
import jax
import jax.numpy as jnp
from jax import lax
from jax.experimental import pallas as pl
from jax.experimental.pallas import tpu as pltpu
from jax.sharding import PartitionSpec as P

KVL = 512
BLOCK = 128
QB = 32
TOPB = 4
OTHERS = TOPB - 1

SCORE_SCALE = 0.07216878364870323
MASKED = -1e30

Z, Y, C = 8, 4, 2
X = 4
Z_FULL = 6
FIRST_OWN_OWNER = Z_FULL * Y * C


F32 = jnp.float32
BF16 = jnp.bfloat16


def seq_of(z, y, c):
    return ((z % Z) * Y + y % Y) * C + c


def shift_z(array, step, sends=lambda z: True):
    pairs = [
        (seq_of(z, y, c), seq_of(z + step, y, c))
        for z in range(Z)
        for y in range(Y)
        for c in range(C)
        if sends(z)
    ]
    return lax.ppermute(array, "seq", pairs)


def gather_z(own, limit):
    right, left = [own], [own]
    for hop in range(4):
        right.append(shift_z(right[-1], 1, lambda z: (z - hop) % Z < limit))
        if hop < 3:
            left.append(shift_z(left[-1], -1, lambda z: (z + hop) % Z < limit))
    return [own, left[1], left[2], left[3], right[4], right[3], right[2], right[1]]


def reduce_z(terms, limit, beside):
    right, left = terms[4], terms[5]
    for hop in range(4):
        right = shift_z(right, 1, lambda z: (z + 4 - hop) % Z < limit)
        if hop < 3:
            left = shift_z(left, -1, lambda z: (z - 3 + hop) % Z < limit)
        if hop == 1:
            right, left, beside = lax.optimization_barrier((right, left, beside))
        if hop < 3:
            right = narrow(wide(right) + wide(terms[3 - hop]))
        if hop < 2:
            left = narrow(wide(left) + wide(terms[6 + hop]))
    return wide(terms[0]) + wide(right) + wide(left), beside


def shift_yc(array, y_step, c_step):
    pairs = [
        (seq_of(z, y, c), seq_of(z, y + y_step, c ^ c_step))
        for z in range(Z)
        for y in range(Y)
        for c in range(C)
    ]
    return lax.ppermute(array, "seq", pairs)


def swap_core(array):
    return lax.ppermute(array, "seq", [(s, s ^ 1) for s in range(Z * Y * C)])


def shift_x(array, step):
    return lax.ppermute(array, "head", [(x, (x + step) % X) for x in range(X)])


def trade(blocks, groups):
    return lax.all_to_all(
        blocks, "seq", split_axis=0, concat_axis=0, axis_index_groups=groups, tiled=True
    )


YC_GROUPS = [[seq_of(z, y, c) for y in range(Y) for c in range(C)] for z in range(Z)]
Y_GROUPS = [[seq_of(z, y, c) for y in range(Y)] for z in range(Z) for c in range(C)]
Z_GROUPS = [[seq_of(z, y, c) for z in range(Z)] for y in range(Y) for c in range(C)]


def narrow(array):
    return array.astype(BF16)


def wide(array):
    return array.astype(F32)


def pack_kernel(block_ref, z_ref, *refs):
    pieces, out_ref = refs[:Z], refs[Z]
    for j in range(Z):
        owner_z = (z_ref[0] + j) % Z

        @pl.when(owner_z < Z_FULL)
        def _():
            for peer in range(Y * C):
                place = peer * Z_FULL + owner_z
                out_ref[place] = pieces[j][block_ref[place]]


def pack(blocks, z, pieces):
    vmem = pl.BlockSpec(memory_space=pltpu.VMEM)
    smem = pl.BlockSpec(memory_space=pltpu.SMEM)
    return pl.pallas_call(
        pack_kernel,
        in_specs=[smem, smem] + [vmem] * Z,
        out_specs=vmem,
        out_shape=jax.ShapeDtypeStruct((blocks.shape[0], *pieces[0].shape[1:]), BF16),
        name="pack",
    )(blocks, z.reshape(1), *pieces)


def pick_kernel(place_ref, own_ref, fetched_ref, *refs):
    owns, (low_ref, high_ref) = refs[:-2], refs[-2:]
    n_low, n_high = low_ref.shape[0], high_ref.shape[0]
    for j, own in enumerate(owns):

        @pl.when(own_ref[0] == j)
        def _():
            low_ref[n_low - 1] = own[...]

    for slot in range(n_low - 1):
        low_ref[slot] = fetched_ref[place_ref[slot]]
    for slot in range(n_high):
        high_ref[slot] = fetched_ref[place_ref[n_low - 1 + slot]]


def pick(place, own_index, fetched, owns):
    vmem = pl.BlockSpec(memory_space=pltpu.VMEM)
    smem = pl.BlockSpec(memory_space=pltpu.SMEM)
    n_high = place.shape[0] // 2
    n_low = place.shape[0] - n_high + 1
    return pl.pallas_call(
        pick_kernel,
        in_specs=[smem, smem, vmem] + [vmem] * len(owns),
        out_specs=[vmem, vmem],
        out_shape=[
            jax.ShapeDtypeStruct((n_low, *fetched.shape[1:]), BF16),
            jax.ShapeDtypeStruct((n_high, *fetched.shape[1:]), BF16),
        ],
        name="pick",
    )(place, own_index.reshape(1), fetched, *owns)


def attend_kernel(x_ref, q_ref, dl_ref, *refs):
    low_refs, own_refs, high_refs = refs[:X], refs[X : 2 * X], refs[2 * X : 3 * X]
    dq_ref, lat_ref = refs[3 * X : 3 * X + 2]
    d_low_refs, d_high_refs = refs[3 * X + 2 : 4 * X + 2], refs[4 * X + 2 : 5 * X + 2]
    keys, own_sum = refs[5 * X + 2 :]
    block = pl.program_id(0)
    half_blocks = pl.num_programs(0) // 2
    rows, width = q_ref.shape
    heads = rows // QB
    quarter = own_refs[0].shape[1]
    n_part = OTHERS * quarter
    n_other = X * n_part

    @pl.when(block < half_blocks)
    def _():
        for j in range(X):
            keys[j * n_part : (j + 1) * n_part] = low_refs[j][...].reshape(n_part, width)

    @pl.when(block >= half_blocks)
    def _():
        for j in range(X):
            keys[j * n_part : (j + 1) * n_part] = high_refs[j][...].reshape(n_part, width)

    @pl.when(block == 0)
    def _():
        for j in range(X):
            keys[n_other + j * quarter : n_other + (j + 1) * quarter] = own_refs[j][0]

    q = q_ref[...]
    dl = dl_ref[...]
    k = keys[...]
    v = keys[:, :KVL]
    n_keys = k.shape[0]
    scores = lax.dot_general(q, k, (((1,), (1,)), ((), ())), preferred_element_type=F32)
    scores = scores * SCORE_SCALE
    col = lax.broadcasted_iota(jnp.int32, (rows, n_keys - n_other), 1)
    row = lax.broadcasted_iota(jnp.int32, (rows, n_keys - n_other), 0)
    source = (x_ref[0] + X - col // quarter) % X
    visible = source * quarter + col % quarter <= block * QB + row // heads
    scores = jnp.concatenate(
        [scores[:, :n_other], jnp.where(visible, scores[:, n_other:], MASKED)], axis=1
    )
    row_max = jnp.max(scores, axis=1, keepdims=True)
    exp_scores = jnp.exp(scores - row_max)
    weights = exp_scores / jnp.sum(exp_scores, axis=1, keepdims=True)
    weights_low = narrow(weights)
    latent = narrow(jnp.dot(weights_low, v, preferred_element_type=F32))
    lat_ref[...] = latent
    delta = jnp.sum(wide(dl) * wide(latent), axis=1, keepdims=True)
    d_probs = lax.dot_general(dl, v, (((1,), (1,)), ((), ())), preferred_element_type=F32)
    d_scores = narrow(SCORE_SCALE * weights * (d_probs - delta))
    dq_ref[...] = narrow(jnp.dot(d_scores, k, preferred_element_type=F32))
    d_keys = lax.dot_general(d_scores, q, (((0,), (0,)), ((), ())), preferred_element_type=F32)
    d_values = lax.dot_general(
        weights_low, dl, (((0,), (0,)), ((), ())), preferred_element_type=F32
    )
    d_keys = jnp.concatenate([d_keys[:, :KVL] + d_values, d_keys[:, KVL:]], axis=1)
    d_other = narrow(d_keys[:n_other]).reshape(X, OTHERS, quarter, width)

    @pl.when(block < half_blocks)
    def _():
        for j in range(X):
            d_low_refs[j][pl.ds(OTHERS * block, OTHERS)] = d_other[j]

    @pl.when(block >= half_blocks)
    def _():
        for j in range(X):
            d_high_refs[j][pl.ds(OTHERS * (block - half_blocks), OTHERS)] = d_other[j]

    d_own = d_keys[n_other:]

    @pl.when(block == 0)
    def _():
        own_sum[...] = d_own

    @pl.when(block > 0)
    def _():
        own_sum[...] += d_own

    @pl.when(block == pl.num_programs(0) - 1)
    def _():
        last = d_low_refs[0].shape[0] - 1
        for j in range(X):
            d_low_refs[j][last] = narrow(own_sum[j * quarter : (j + 1) * quarter])


def attend(x, q, dl, low, high, interpret=False):
    rows, width = q.shape
    n_low, quarter, _ = low[0].shape
    n_high = high[0].shape[0]
    blocks = (n_low - 1 + n_high) // OTHERS
    half = blocks // 2
    per = rows // blocks
    n_keys = TOPB * X * quarter
    part = (OTHERS, quarter, width)
    return pl.pallas_call(
        attend_kernel,
        grid_spec=pltpu.PrefetchScalarGridSpec(
            num_scalar_prefetch=1,
            grid=(blocks,),
            in_specs=[
                pl.BlockSpec((per, width), lambda g, x: (g, 0)),
                pl.BlockSpec((per, KVL), lambda g, x: (g, 0)),
            ]
            + [pl.BlockSpec(part, lambda g, x: (jnp.minimum(g, half - 1), 0, 0))] * X
            + [pl.BlockSpec((1, quarter, width), lambda g, x: (n_low - 1, 0, 0))] * X
            + [pl.BlockSpec(part, lambda g, x: (jnp.maximum(g - half, 0), 0, 0))] * X,
            out_specs=[
                pl.BlockSpec((per, width), lambda g, x: (g, 0)),
                pl.BlockSpec((per, KVL), lambda g, x: (g, 0)),
            ]
            + [pl.BlockSpec((n_low, quarter, width), lambda g, x: (0, 0, 0))] * X
            + [pl.BlockSpec((n_high, quarter, width), lambda g, x: (0, 0, 0))] * X,
            scratch_shapes=[
                pltpu.VMEM((n_keys, width), BF16),
                pltpu.VMEM((X * quarter, width), F32),
            ],
        ),
        out_shape=[
            jax.ShapeDtypeStruct((rows, width), BF16),
            jax.ShapeDtypeStruct((rows, KVL), BF16),
        ]
        + [jax.ShapeDtypeStruct((n_low, quarter, width), BF16)] * X
        + [jax.ShapeDtypeStruct((n_high, quarter, width), BF16)] * X,
        interpret=interpret,
        compiler_params=pltpu.CompilerParams(vmem_limit_bytes=56 * 2**20),
        name="attend",
    )(x.reshape(1), q, dl, *low, *low, *high)


def send_back_kernel(at_ref, *refs):
    low_refs, high_refs = refs[:3], refs[3:6]
    out_refs, own_ref, total = refs[6:-2], refs[-2], refs[-1]
    n_low, n_high = low_refs[0].shape[0], high_refs[0].shape[0]
    total[...] = jnp.zeros_like(total)
    for slot in range(n_low + n_high - 1):
        refs_here, index = (low_refs, slot) if slot < n_low - 1 else (high_refs, slot - n_low + 1)
        share = wide(refs_here[0][index]) + wide(refs_here[1][index]) + wide(refs_here[2][index])
        total[at_ref[slot]] += share
    last = n_low - 1
    own_ref[...] = narrow(
        wide(low_refs[0][last]) + wide(low_refs[1][last]) + wide(low_refs[2][last])
    )
    for j, out_ref in enumerate(out_refs):
        out_ref[...] = narrow(total[j * Z_FULL : (j + 1) * Z_FULL])


def send_back(at, low, high):
    _, quarter, width = low[0].shape
    vmem = pl.BlockSpec(memory_space=pltpu.VMEM)
    return pl.pallas_call(
        send_back_kernel,
        in_specs=[pl.BlockSpec(memory_space=pltpu.SMEM)] + [vmem] * 6,
        out_specs=[vmem] * (Y * C + 1),
        out_shape=[jax.ShapeDtypeStruct((Z_FULL, quarter, width), BF16)] * (Y * C)
        + [jax.ShapeDtypeStruct((quarter, width), BF16)],
        scratch_shapes=[pltpu.VMEM((Y * C * Z_FULL, quarter, width), F32)],
        compiler_params=pltpu.CompilerParams(vmem_limit_bytes=12 * 2**20),
        name="send_back",
    )(at, *low, *high)


FIRST_TERMS = (4, 5)
LATER_TERMS = (0, 1, 2, 3, 6, 7)


def by_owner_kernel(at_ref, *refs):
    in_refs, first_refs, later_ref, total = refs[: Y * C], refs[Y * C : -2], refs[-2], refs[-1]
    total[...] = jnp.zeros_like(total)
    for i, in_ref in enumerate(in_refs):
        for slot in range(Z_FULL):
            total[at_ref[i * Z_FULL + slot]] += wide(in_ref[slot])
    blocks = later_ref.shape[1]
    for j, out_ref in zip(FIRST_TERMS, first_refs):
        out_ref[...] = narrow(total[j * blocks : (j + 1) * blocks])
    for i, j in enumerate(LATER_TERMS):
        later_ref[i] = narrow(total[j * blocks : (j + 1) * blocks])


def by_owner(at, received, blocks):
    _, quarter, width = received[0].shape
    vmem = pl.BlockSpec(memory_space=pltpu.VMEM)
    *first, later = pl.pallas_call(
        by_owner_kernel,
        in_specs=[pl.BlockSpec(memory_space=pltpu.SMEM)] + [vmem] * (Y * C),
        out_specs=[vmem] * (len(FIRST_TERMS) + 1),
        out_shape=[jax.ShapeDtypeStruct((blocks, quarter, width), BF16)] * len(FIRST_TERMS)
        + [jax.ShapeDtypeStruct((len(LATER_TERMS), blocks, quarter, width), BF16)],
        scratch_shapes=[pltpu.VMEM((Z * blocks + 1, quarter, width), F32)],
        compiler_params=pltpu.CompilerParams(vmem_limit_bytes=12 * 2**20),
        name="by_owner",
    )(at, *received)
    terms = [None] * Z
    for j, term in zip(FIRST_TERMS, first):
        terms[j] = term
    for i, j in enumerate(LATER_TERMS):
        terms[j] = later[i]
    return terms


def local(query, cache, grad_out, value_weight, picked):
    q_dev, heads_here, width = query.shape
    block_count = cache.shape[0] // BLOCK
    seq = lax.axis_index("seq")
    x = lax.axis_index("head")
    z, y, c = seq // (Y * C), seq // C % Y, seq % C
    peers = Y * C
    quarter = BLOCK // X
    g_here = q_dev // QB
    others = g_here * OTHERS
    rows = q_dev * heads_here

    own_id = FIRST_OWN_OWNER * block_count + seq
    is_other = picked != own_id
    rank = jnp.cumsum(is_other.astype(jnp.int32), axis=1) - 1
    at_rank = is_other[:, :, None] & (rank[:, :, None] == jnp.arange(OTHERS, dtype=jnp.int32))
    ids = jnp.sum(jnp.where(at_rank, picked[:, :, None], 0), axis=1).reshape(others)
    owner, block = ids // block_count, ids % block_count
    place = owner % peers * Z_FULL + owner // peers
    places = peers * Z_FULL
    asked = place[:, None] == jnp.arange(places, dtype=jnp.int32)[None, :]
    wanted = jnp.max(jnp.where(asked, block[:, None], -1), axis=0)
    asked_here = trade(wanted.reshape(peers, 1, Z_FULL), YC_GROUPS).reshape(peers, Z_FULL)
    z_off = (jnp.arange(Z_FULL, dtype=jnp.int32) - z) % Z
    distance = jnp.arange(peers, dtype=jnp.int32)
    from_peer = (y - distance // C) % Y * C + (c ^ distance % C)
    pick_peer = from_peer[:, None, None] == jnp.arange(peers, dtype=jnp.int32)[None, :, None]
    asked_from = jnp.sum(jnp.where(pick_peer, asked_here[None], 0), axis=1)
    at_owner = jnp.where(
        asked_from >= 0, z_off[None, :] * block_count + asked_from, Z * block_count
    ).reshape(places)
    place_back = (owner // C % Y - y) % Y * C + (owner % C ^ c)
    place_back = place_back * Z_FULL + owner // peers

    part_rows = jnp.arange(block_count * quarter, dtype=jnp.int32)
    part_rows = part_rows // quarter * BLOCK + x * quarter + part_rows % quarter
    take_part = part_rows[:, None] == jnp.arange(cache.shape[0], dtype=jnp.int32)[None, :]
    part = jnp.dot(take_part.astype(BF16), cache, preferred_element_type=F32)
    part = narrow(part).reshape(block_count, quarter, width)
    pieces = gather_z(part, Z_FULL)
    owns = []
    for j in range(block_count):
        owns.append(
            lax.ppermute(
                part[j],
                "seq",
                [
                    (o, (o - FIRST_OWN_OWNER) * block_count + j)
                    for o in range(FIRST_OWN_OWNER, Z * peers)
                ],
            )
        )
    packed = pack(jnp.maximum(asked_here, 0).reshape(places), z, pieces)
    fetched = trade(packed.reshape(peers, Z_FULL, quarter, width), YC_GROUPS)
    d_latent = narrow(
        jnp.einsum("qhv,hcv->qhc", grad_out, value_weight, preferred_element_type=F32)
    )
    fetched, d_latent, query_rows = lax.optimization_barrier(
        (fetched, d_latent.reshape(rows, KVL), query.reshape(rows, width))
    )
    low, high = pick(place, seq % block_count, fetched.reshape(places, quarter, width), owns)

    low_from_left = shift_x(low, 1)
    high_from_right = shift_x(high, -1)
    low_from_right = shift_x(low, -1)
    high_from_left = shift_x(high, 1)
    low_far = shift_x(low_from_left, 1)
    high_far = shift_x(high_from_right, -1)

    d_query, latent_out, *d_keys = attend(
        x,
        query_rows,
        d_latent,
        [low, low_from_left, low_far, low_from_right],
        [high, high_from_left, high_far, high_from_right],
    )
    d_low, d_high = d_keys[:X], d_keys[X:]

    low_relay = shift_x(d_low[2], -1)
    high_relay = shift_x(d_high[2], 1)
    high_left = shift_x(d_high[1], -1)
    low_right = shift_x(d_low[3], 1)
    low_pair = narrow(wide(low_relay) + wide(d_low[1]))
    high_pair = narrow(wide(high_relay) + wide(d_high[3]))
    low_left = shift_x(low_pair, -1)
    high_right = shift_x(high_pair, 1)

    terms = narrow(
        jnp.einsum(
            "qhc,qhv->hcv",
            latent_out.reshape(q_dev, heads_here, KVL),
            grad_out,
            preferred_element_type=F32,
        )
    )
    v_dim = terms.shape[-1]
    terms = terms.reshape(Y, C, -1, v_dim)
    arrived = swap_core(lax.dynamic_index_in_dim(terms, 1 - c, 1, keepdims=False))
    terms = lax.dynamic_index_in_dim(terms, c, 1, keepdims=False)
    terms = narrow(wide(terms) + wide(arrived))
    terms = trade(terms, Y_GROUPS)
    terms = narrow(jnp.sum(wide(terms), axis=0))
    terms = trade(terms.reshape(Z, -1, v_dim), Z_GROUPS)
    terms = narrow(jnp.sum(wide(terms), axis=0))
    terms = trade(jnp.broadcast_to(terms, (Z, *terms.shape)), Z_GROUPS).reshape(-1, v_dim)
    terms = trade(jnp.broadcast_to(terms, (peers, *terms.shape)), YC_GROUPS)
    d_value_weight = terms.reshape(value_weight.shape)

    *back, own_share = send_back(
        place_back, [d_low[0], low_right, low_left], [d_high[0], high_left, high_right]
    )
    received = [back[0]] + [None] * (peers - 1)
    for i in (5, 4, 3, 7, 2, 6, 1):
        received[i] = shift_yc(back[i], i // C, i % C)
    own_back = []
    for j in range(block_count):
        own_back.append(
            lax.ppermute(
                own_share,
                "seq",
                [
                    ((o - FIRST_OWN_OWNER) * block_count + j, o)
                    for o in range(FIRST_OWN_OWNER, Z * peers)
                ],
            )
        )
    d_query = jnp.transpose(d_query.reshape(query.shape), (1, 2, 0))
    by_z = by_owner(at_owner, received, block_count)
    d_cache, d_query = reduce_z(by_z, Z_FULL, d_query)
    d_cache = d_cache + wide(jnp.stack(own_back))
    return jnp.transpose(d_query, (2, 0, 1)), d_cache, d_value_weight


def solution(mesh):
    in_specs = (
        P("seq", "head", None),
        P("seq", None),
        P("seq", "head", None),
        P("head", None, None),
        P("seq", None),
    )
    out_specs = (P("seq", "head", None), P("seq", "head", None), P("head", None, None))
    return jax.shard_map(local, mesh=mesh, in_specs=in_specs, out_specs=out_specs, check_vma=False)
```

```python
import jax
import jax.numpy as jnp
from jax import lax
from jax.experimental import pallas as pl
from jax.experimental.pallas import tpu as pltpu
from jax.sharding import PartitionSpec as P

KVL = 512
BLOCK = 128
QB = 32
TOPB = 4
OTHERS = TOPB - 1

SCORE_SCALE = 0.07216878364870323
MASKED = -1e30

Z, Y, C = 8, 4, 2
X = 4
Z_FULL = 6
FIRST_OWN_OWNER = Z_FULL * Y * C


F32 = jnp.float32
BF16 = jnp.bfloat16


def seq_of(z, y, c):
    return ((z % Z) * Y + y % Y) * C + c


def shift_z(array, step, sends=lambda z: True):
    pairs = [
        (seq_of(z, y, c), seq_of(z + step, y, c))
        for z in range(Z)
        for y in range(Y)
        for c in range(C)
        if sends(z)
    ]
    return lax.ppermute(array, "seq", pairs)


def gather_z(own, limit):
    right, left = [own], [own]
    for hop in range(4):
        right.append(shift_z(right[-1], 1, lambda z: (z - hop) % Z < limit))
        if hop < 3:
            left.append(shift_z(left[-1], -1, lambda z: (z + hop) % Z < limit))
    return [own, left[1], left[2], left[3], right[4], right[3], right[2], right[1]]


def reduce_z(terms, limit, beside):
    right, left = terms[4], terms[5]
    for hop in range(4):
        right = shift_z(right, 1, lambda z: (z + 4 - hop) % Z < limit)
        if hop < 3:
            left = shift_z(left, -1, lambda z: (z - 3 + hop) % Z < limit)
        if hop == 1:
            right, left, beside = lax.optimization_barrier((right, left, beside))
        if hop < 3:
            right = narrow(wide(right) + wide(terms[3 - hop]))
        if hop < 2:
            left = narrow(wide(left) + wide(terms[6 + hop]))
    return wide(terms[0]) + wide(right) + wide(left), beside


def shift_yc(array, y_step, c_step):
    pairs = [
        (seq_of(z, y, c), seq_of(z, y + y_step, c ^ c_step))
        for z in range(Z)
        for y in range(Y)
        for c in range(C)
    ]
    return lax.ppermute(array, "seq", pairs)


def swap_core(array):
    return lax.ppermute(array, "seq", [(s, s ^ 1) for s in range(Z * Y * C)])


def shift_x(array, step):
    return lax.ppermute(array, "head", [(x, (x + step) % X) for x in range(X)])


def trade(blocks, groups):
    return lax.all_to_all(
        blocks, "seq", split_axis=0, concat_axis=0, axis_index_groups=groups, tiled=True
    )


YC_GROUPS = [[seq_of(z, y, c) for y in range(Y) for c in range(C)] for z in range(Z)]
Y_GROUPS = [[seq_of(z, y, c) for y in range(Y)] for z in range(Z) for c in range(C)]
Z_GROUPS = [[seq_of(z, y, c) for z in range(Z)] for y in range(Y) for c in range(C)]


def narrow(array):
    return array.astype(BF16)


def wide(array):
    return array.astype(F32)


def pack_kernel(block_ref, z_ref, *refs):
    pieces, out_ref = refs[:Z], refs[Z]
    for j in range(Z):
        owner_z = (z_ref[0] + j) % Z

        @pl.when(owner_z < Z_FULL)
        def _():
            for peer in range(Y * C):
                place = peer * Z_FULL + owner_z
                out_ref[place] = pieces[j][block_ref[place]]


def pack(blocks, z, pieces):
    vmem = pl.BlockSpec(memory_space=pltpu.VMEM)
    smem = pl.BlockSpec(memory_space=pltpu.SMEM)
    return pl.pallas_call(
        pack_kernel,
        in_specs=[smem, smem] + [vmem] * Z,
        out_specs=vmem,
        out_shape=jax.ShapeDtypeStruct((blocks.shape[0], *pieces[0].shape[1:]), BF16),
        name="pack",
    )(blocks, z.reshape(1), *pieces)


def pick_kernel(place_ref, own_ref, fetched_ref, *refs):
    owns, (low_ref, high_ref) = refs[:-2], refs[-2:]
    n_low, n_high = low_ref.shape[0], high_ref.shape[0]
    for j, own in enumerate(owns):

        @pl.when(own_ref[0] == j)
        def _():
            low_ref[n_low - 1] = own[...]

    for slot in range(n_low - 1):
        low_ref[slot] = fetched_ref[place_ref[slot]]
    for slot in range(n_high):
        high_ref[slot] = fetched_ref[place_ref[n_low - 1 + slot]]


def pick(place, own_index, fetched, owns):
    vmem = pl.BlockSpec(memory_space=pltpu.VMEM)
    smem = pl.BlockSpec(memory_space=pltpu.SMEM)
    n_high = place.shape[0] // 2
    n_low = place.shape[0] - n_high + 1
    return pl.pallas_call(
        pick_kernel,
        in_specs=[smem, smem, vmem] + [vmem] * len(owns),
        out_specs=[vmem, vmem],
        out_shape=[
            jax.ShapeDtypeStruct((n_low, *fetched.shape[1:]), BF16),
            jax.ShapeDtypeStruct((n_high, *fetched.shape[1:]), BF16),
        ],
        name="pick",
    )(place, own_index.reshape(1), fetched, *owns)


def attend_kernel(x_ref, q_ref, dl_ref, *refs):
    low_refs, own_refs, high_refs = refs[:X], refs[X : 2 * X], refs[2 * X : 3 * X]
    dq_ref, lat_ref = refs[3 * X : 3 * X + 2]
    d_low_refs, d_high_refs = refs[3 * X + 2 : 4 * X + 2], refs[4 * X + 2 : 5 * X + 2]
    keys, own_sum = refs[5 * X + 2 :]
    block = pl.program_id(0)
    half_blocks = pl.num_programs(0) // 2
    rows, width = q_ref.shape
    heads = rows // QB
    quarter = own_refs[0].shape[1]
    n_part = OTHERS * quarter
    n_other = X * n_part

    @pl.when(block < half_blocks)
    def _():
        for j in range(X):
            keys[j * n_part : (j + 1) * n_part] = low_refs[j][...].reshape(n_part, width)

    @pl.when(block >= half_blocks)
    def _():
        for j in range(X):
            keys[j * n_part : (j + 1) * n_part] = high_refs[j][...].reshape(n_part, width)

    @pl.when(block == 0)
    def _():
        for j in range(X):
            keys[n_other + j * quarter : n_other + (j + 1) * quarter] = own_refs[j][0]

    q = q_ref[...]
    dl = dl_ref[...]
    k = keys[...]
    v = keys[:, :KVL]
    n_keys = k.shape[0]
    scores = lax.dot_general(q, k, (((1,), (1,)), ((), ())), preferred_element_type=F32)
    scores = scores * SCORE_SCALE
    col = lax.broadcasted_iota(jnp.int32, (rows, n_keys - n_other), 1)
    row = lax.broadcasted_iota(jnp.int32, (rows, n_keys - n_other), 0)
    source = (x_ref[0] + X - col // quarter) % X
    visible = source * quarter + col % quarter <= block * QB + row // heads
    scores = jnp.concatenate(
        [scores[:, :n_other], jnp.where(visible, scores[:, n_other:], MASKED)], axis=1
    )
    row_max = jnp.max(scores, axis=1, keepdims=True)
    exp_scores = jnp.exp(scores - row_max)
    weights = exp_scores / jnp.sum(exp_scores, axis=1, keepdims=True)
    weights_low = narrow(weights)
    latent = narrow(jnp.dot(weights_low, v, preferred_element_type=F32))
    lat_ref[...] = latent
    delta = jnp.sum(wide(dl) * wide(latent), axis=1, keepdims=True)
    d_probs = lax.dot_general(dl, v, (((1,), (1,)), ((), ())), preferred_element_type=F32)
    d_scores = narrow(SCORE_SCALE * weights * (d_probs - delta))
    dq_ref[...] = narrow(jnp.dot(d_scores, k, preferred_element_type=F32))
    d_keys = lax.dot_general(d_scores, q, (((0,), (0,)), ((), ())), preferred_element_type=F32)
    d_values = lax.dot_general(
        weights_low, dl, (((0,), (0,)), ((), ())), preferred_element_type=F32
    )
    d_keys = jnp.concatenate([d_keys[:, :KVL] + d_values, d_keys[:, KVL:]], axis=1)
    d_other = narrow(d_keys[:n_other]).reshape(X, OTHERS, quarter, width)

    @pl.when(block < half_blocks)
    def _():
        for j in range(X):
            d_low_refs[j][pl.ds(OTHERS * block, OTHERS)] = d_other[j]

    @pl.when(block >= half_blocks)
    def _():
        for j in range(X):
            d_high_refs[j][pl.ds(OTHERS * (block - half_blocks), OTHERS)] = d_other[j]

    d_own = d_keys[n_other:]

    @pl.when(block == 0)
    def _():
        own_sum[...] = d_own

    @pl.when(block > 0)
    def _():
        own_sum[...] += d_own

    @pl.when(block == pl.num_programs(0) - 1)
    def _():
        last = d_low_refs[0].shape[0] - 1
        for j in range(X):
            d_low_refs[j][last] = narrow(own_sum[j * quarter : (j + 1) * quarter])


def attend(x, q, dl, low, high, interpret=False):
    rows, width = q.shape
    n_low, quarter, _ = low[0].shape
    n_high = high[0].shape[0]
    blocks = (n_low - 1 + n_high) // OTHERS
    half = blocks // 2
    per = rows // blocks
    n_keys = TOPB * X * quarter
    part = (OTHERS, quarter, width)
    return pl.pallas_call(
        attend_kernel,
        grid_spec=pltpu.PrefetchScalarGridSpec(
            num_scalar_prefetch=1,
            grid=(blocks,),
            in_specs=[
                pl.BlockSpec((per, width), lambda g, x: (g, 0)),
                pl.BlockSpec((per, KVL), lambda g, x: (g, 0)),
            ]
            + [pl.BlockSpec(part, lambda g, x: (jnp.minimum(g, half - 1), 0, 0))] * X
            + [pl.BlockSpec((1, quarter, width), lambda g, x: (n_low - 1, 0, 0))] * X
            + [pl.BlockSpec(part, lambda g, x: (jnp.maximum(g - half, 0), 0, 0))] * X,
            out_specs=[
                pl.BlockSpec((per, width), lambda g, x: (g, 0)),
                pl.BlockSpec((per, KVL), lambda g, x: (g, 0)),
            ]
            + [pl.BlockSpec((n_low, quarter, width), lambda g, x: (0, 0, 0))] * X
            + [pl.BlockSpec((n_high, quarter, width), lambda g, x: (0, 0, 0))] * X,
            scratch_shapes=[
                pltpu.VMEM((n_keys, width), BF16),
                pltpu.VMEM((X * quarter, width), F32),
            ],
        ),
        out_shape=[
            jax.ShapeDtypeStruct((rows, width), BF16),
            jax.ShapeDtypeStruct((rows, KVL), BF16),
        ]
        + [jax.ShapeDtypeStruct((n_low, quarter, width), BF16)] * X
        + [jax.ShapeDtypeStruct((n_high, quarter, width), BF16)] * X,
        interpret=interpret,
        compiler_params=pltpu.CompilerParams(vmem_limit_bytes=56 * 2**20),
        name="attend",
    )(x.reshape(1), q, dl, *low, *low, *high)


def send_back_kernel(at_ref, *refs):
    low_refs, high_refs = refs[:3], refs[3:6]
    out_refs, own_ref, total = refs[6:-2], refs[-2], refs[-1]
    n_low, n_high = low_refs[0].shape[0], high_refs[0].shape[0]
    total[...] = jnp.zeros_like(total)
    for slot in range(n_low + n_high - 1):
        refs_here, index = (low_refs, slot) if slot < n_low - 1 else (high_refs, slot - n_low + 1)
        share = wide(refs_here[0][index]) + wide(refs_here[1][index]) + wide(refs_here[2][index])
        total[at_ref[slot]] += share
    last = n_low - 1
    own_ref[...] = narrow(
        wide(low_refs[0][last]) + wide(low_refs[1][last]) + wide(low_refs[2][last])
    )
    for j, out_ref in enumerate(out_refs):
        out_ref[...] = narrow(total[j * Z_FULL : (j + 1) * Z_FULL])


def send_back(at, low, high):
    _, quarter, width = low[0].shape
    vmem = pl.BlockSpec(memory_space=pltpu.VMEM)
    return pl.pallas_call(
        send_back_kernel,
        in_specs=[pl.BlockSpec(memory_space=pltpu.SMEM)] + [vmem] * 6,
        out_specs=[vmem] * (Y * C + 1),
        out_shape=[jax.ShapeDtypeStruct((Z_FULL, quarter, width), BF16)] * (Y * C)
        + [jax.ShapeDtypeStruct((quarter, width), BF16)],
        scratch_shapes=[pltpu.VMEM((Y * C * Z_FULL, quarter, width), F32)],
        compiler_params=pltpu.CompilerParams(vmem_limit_bytes=40 * 2**20),
        name="send_back",
    )(at, *low, *high)


def by_owner_kernel(at_ref, *refs):
    in_refs, out_refs, total = refs[: Y * C], refs[Y * C : -1], refs[-1]
    total[...] = jnp.zeros_like(total)
    for i, in_ref in enumerate(in_refs):
        for slot in range(Z_FULL):
            total[at_ref[i * Z_FULL + slot]] += wide(in_ref[slot])
    blocks = out_refs[0].shape[0]
    for j, out_ref in enumerate(out_refs):
        out_ref[...] = narrow(total[j * blocks : (j + 1) * blocks])


def by_owner(at, received, blocks):
    _, quarter, width = received[0].shape
    vmem = pl.BlockSpec(memory_space=pltpu.VMEM)
    return pl.pallas_call(
        by_owner_kernel,
        in_specs=[pl.BlockSpec(memory_space=pltpu.SMEM)] + [vmem] * (Y * C),
        out_specs=[vmem] * Z,
        out_shape=[jax.ShapeDtypeStruct((blocks, quarter, width), BF16)] * Z,
        scratch_shapes=[pltpu.VMEM((Z * blocks + 1, quarter, width), F32)],
        compiler_params=pltpu.CompilerParams(vmem_limit_bytes=40 * 2**20),
        name="by_owner",
    )(at, *received)


def local(query, cache, grad_out, value_weight, picked):
    q_dev, heads_here, width = query.shape
    block_count = cache.shape[0] // BLOCK
    seq = lax.axis_index("seq")
    x = lax.axis_index("head")
    z, y, c = seq // (Y * C), seq // C % Y, seq % C
    peers = Y * C
    quarter = BLOCK // X
    g_here = q_dev // QB
    others = g_here * OTHERS
    rows = q_dev * heads_here

    own_id = FIRST_OWN_OWNER * block_count + seq
    is_other = picked != own_id
    rank = jnp.cumsum(is_other.astype(jnp.int32), axis=1) - 1
    at_rank = is_other[:, :, None] & (rank[:, :, None] == jnp.arange(OTHERS, dtype=jnp.int32))
    ids = jnp.sum(jnp.where(at_rank, picked[:, :, None], 0), axis=1).reshape(others)
    owner, block = ids // block_count, ids % block_count
    place = owner % peers * Z_FULL + owner // peers
    places = peers * Z_FULL
    asked = place[:, None] == jnp.arange(places, dtype=jnp.int32)[None, :]
    wanted = jnp.max(jnp.where(asked, block[:, None], -1), axis=0)
    asked_here = trade(wanted.reshape(peers, 1, Z_FULL), YC_GROUPS).reshape(peers, Z_FULL)
    z_off = (jnp.arange(Z_FULL, dtype=jnp.int32) - z) % Z
    distance = jnp.arange(peers, dtype=jnp.int32)
    from_peer = (y - distance // C) % Y * C + (c ^ distance % C)
    pick_peer = from_peer[:, None, None] == jnp.arange(peers, dtype=jnp.int32)[None, :, None]
    asked_from = jnp.sum(jnp.where(pick_peer, asked_here[None], 0), axis=1)
    at_owner = jnp.where(
        asked_from >= 0, z_off[None, :] * block_count + asked_from, Z * block_count
    ).reshape(places)
    place_back = (owner // C % Y - y) % Y * C + (owner % C ^ c)
    place_back = place_back * Z_FULL + owner // peers

    part_rows = jnp.arange(block_count * quarter, dtype=jnp.int32)
    part_rows = part_rows // quarter * BLOCK + x * quarter + part_rows % quarter
    take_part = part_rows[:, None] == jnp.arange(cache.shape[0], dtype=jnp.int32)[None, :]
    part = jnp.dot(take_part.astype(BF16), cache, preferred_element_type=F32)
    part = narrow(part).reshape(block_count, quarter, width)
    pieces = gather_z(part, Z_FULL)
    owns = []
    for j in range(block_count):
        owns.append(
            lax.ppermute(
                part[j],
                "seq",
                [
                    (o, (o - FIRST_OWN_OWNER) * block_count + j)
                    for o in range(FIRST_OWN_OWNER, Z * peers)
                ],
            )
        )
    packed = pack(jnp.maximum(asked_here, 0).reshape(places), z, pieces)
    fetched = trade(packed.reshape(peers, Z_FULL, quarter, width), YC_GROUPS)
    d_latent = narrow(
        jnp.einsum("qhv,hcv->qhc", grad_out, value_weight, preferred_element_type=F32)
    )
    fetched, d_latent, query_rows = lax.optimization_barrier(
        (fetched, d_latent.reshape(rows, KVL), query.reshape(rows, width))
    )
    low, high = pick(place, seq % block_count, fetched.reshape(places, quarter, width), owns)

    low_from_left = shift_x(low, 1)
    high_from_right = shift_x(high, -1)
    low_from_right = shift_x(low, -1)
    high_from_left = shift_x(high, 1)
    low_far = shift_x(low_from_left, 1)
    high_far = shift_x(high_from_right, -1)

    d_query, latent_out, *d_keys = attend(
        x,
        query_rows,
        d_latent,
        [low, low_from_left, low_far, low_from_right],
        [high, high_from_left, high_far, high_from_right],
    )
    d_low, d_high = d_keys[:X], d_keys[X:]

    low_relay = shift_x(d_low[2], -1)
    high_relay = shift_x(d_high[2], 1)
    high_left = shift_x(d_high[1], -1)
    low_right = shift_x(d_low[3], 1)
    low_pair = narrow(wide(low_relay) + wide(d_low[1]))
    high_pair = narrow(wide(high_relay) + wide(d_high[3]))
    low_left = shift_x(low_pair, -1)
    high_right = shift_x(high_pair, 1)

    terms = narrow(
        jnp.einsum(
            "qhc,qhv->hcv",
            latent_out.reshape(q_dev, heads_here, KVL),
            grad_out,
            preferred_element_type=F32,
        )
    )
    v_dim = terms.shape[-1]
    terms = terms.reshape(Y, C, -1, v_dim)
    arrived = swap_core(lax.dynamic_index_in_dim(terms, 1 - c, 1, keepdims=False))
    terms = lax.dynamic_index_in_dim(terms, c, 1, keepdims=False)
    terms = narrow(wide(terms) + wide(arrived))
    terms = trade(terms, Y_GROUPS)
    terms = narrow(jnp.sum(wide(terms), axis=0))
    terms = trade(terms.reshape(Z, -1, v_dim), Z_GROUPS)
    terms = narrow(jnp.sum(wide(terms), axis=0))
    terms = trade(jnp.broadcast_to(terms, (Z, *terms.shape)), Z_GROUPS).reshape(-1, v_dim)
    terms = trade(jnp.broadcast_to(terms, (peers, *terms.shape)), YC_GROUPS)
    d_value_weight = terms.reshape(value_weight.shape)

    *back, own_share = send_back(
        place_back, [d_low[0], low_right, low_left], [d_high[0], high_left, high_right]
    )
    received = [back[0]] + [None] * (peers - 1)
    for i in (5, 4, 3, 7, 2, 6, 1):
        received[i] = shift_yc(back[i], i // C, i % C)
    own_back = []
    for j in range(block_count):
        own_back.append(
            lax.ppermute(
                own_share,
                "seq",
                [
                    ((o - FIRST_OWN_OWNER) * block_count + j, o)
                    for o in range(FIRST_OWN_OWNER, Z * peers)
                ],
            )
        )
    d_query = jnp.transpose(d_query.reshape(query.shape), (1, 2, 0))
    by_z = by_owner(at_owner, received, block_count)
    d_cache, d_query = reduce_z(by_z, Z_FULL, d_query)
    d_cache = d_cache + wide(jnp.stack(own_back))
    return jnp.transpose(d_query, (2, 0, 1)), d_cache, d_value_weight


def solution(mesh):
    in_specs = (
        P("seq", "head", None),
        P("seq", None),
        P("seq", "head", None),
        P("head", None, None),
        P("seq", None),
    )
    out_specs = (P("seq", "head", None), P("seq", "head", None), P("head", None, None))
    return jax.shard_map(local, mesh=mesh, in_specs=in_specs, out_specs=out_specs, check_vma=False)
```
